128 devices in a mesh: energy: 32 (over y, z_lo, x), blk: 4 (over z_hi, core).
Axes of the slice: x: 4, y: 4, z: 4 (z_hi: 2, z_lo: 2; z = z_hi * 2 + z_lo), core: 2. Of those that a mesh axis runs over, the one named last changes fastest.
Arguments:
- lesser_green: bfloat16 [64, 4, 2, 384, 384], P('energy', 'blk'), may hold values from -4.1875 to 4.1875
- greater_green: bfloat16 [64, 4, 2, 384, 384], P('energy', 'blk'), may hold values from -4.1875 to 4.1875
- coulomb_blocks: bfloat16 [4, 3, 2, 384, 384], P('blk'), may hold values from -0.21875 to 0.21875
Outputs:
- lesser_sigma: bfloat16 [64, 4, 2, 384, 384], P('energy', 'blk')
- greater_sigma: bfloat16 [64, 4, 2, 384, 384], P('energy', 'blk')
The draws below stay inside these ranges and needn't reach their ends.
All inputs are finite; a program needn't handle non-finite values.
Results may differ from the reference program's by a relative error of at most 0.017.
Values may be sent and summed in bfloat16 or wider, within the bound.
A program may use at most 128 MiB of HBM per device.

```python
import math
import jax
import jax.numpy as jnp
from jax import lax

M = 384
NE = 64
BLOCKS = 4


def shard_levels(own_key, shape, split, low, high):
    loudness = 1.0
    for dim, parts in split:
        draws = jax.random.uniform(jax.random.fold_in(jax.random.fold_in(own_key, 6), dim), (parts,), jnp.float32, low / len(split), high / len(split))
        loudness = loudness * jnp.repeat(jnp.exp(draws), shape[dim] // parts).reshape((-1,) + (1,) * (len(shape) - 1 - dim))
    return loudness


def bell_draw(stream_key, extent, spread, limit, shards=(), dtype=jnp.bfloat16):
    entries = spread * jax.random.normal(stream_key, extent, jnp.float32)
    if shards:
        entries = entries * shard_levels(stream_key, extent, shards, -0.22, 0.18)
    return jnp.clip(entries, -limit, limit).astype(dtype)


def setup_inputs(seed: int = 0) -> dict:
    streams_of = jax.random.split(jax.random.key(seed), 4)
    lesser_green = bell_draw(streams_of[0], (NE, BLOCKS, 2, M, M), 0.7, 4.1875, ((0, 32), (1, 4)))
    greater_green = bell_draw(streams_of[1], (NE, BLOCKS, 2, M, M), 0.7, 4.1875, ((0, 32), (1, 4)))
    coulomb_blocks = bell_draw(streams_of[2], (BLOCKS, 3, 2, M, M), (2 * M) ** -0.5, 0.21875, ((0, 4),))
    return {"lesser_green": lesser_green, "greater_green": greater_green, "coulomb_blocks": coulomb_blocks}


top_precision = lax.Precision.HIGHEST

def as_complex(pair):
    return pair[:, 0].astype(jnp.float32) + 1j * pair[:, 1].astype(jnp.float32)

def as_pair(values):
    return jnp.stack([jnp.real(values), jnp.imag(values)], axis=1).astype(jnp.bfloat16)

def product(first, second, form):
    return jnp.einsum(form, first, second, precision=top_precision)

def rounded(values):
    return lax.optimization_barrier(values.astype(jnp.bfloat16)).astype(jnp.float32)

def congruence(coupling, polar):
    coul_re = coupling[0].astype(jnp.float32)
    coul_im = coupling[1].astype(jnp.float32)
    pol_re = polar[:, 0].astype(jnp.float32)
    pol_im = polar[:, 1].astype(jnp.float32)
    left_re = rounded(product(coul_re, pol_re, 'ij,ejk->eik') - product(coul_im, pol_im, 'ij,ejk->eik'))
    left_im = rounded(product(coul_re, pol_im, 'ij,ejk->eik') + product(coul_im, pol_re, 'ij,ejk->eik'))
    right_re = product(left_re, coul_re, 'eik,jk->eij') + product(left_im, coul_im, 'eik,jk->eij')
    right_im = product(left_im, coul_re, 'eik,jk->eij') - product(left_re, coul_im, 'eik,jk->eij')
    return (right_re, right_im)

def reference(lesser_green, greater_green, coulomb_blocks):
    length = 2 * NE
    factor = 1.0 / math.sqrt(NE)
    less_specs = []
    great_specs = []
    pol_less = []
    pol_great = []
    for block in range(BLOCKS):
        less_spec = jnp.fft.fft(as_complex(lesser_green[:, block]), n=length, axis=0)
        great_spec = jnp.fft.fft(as_complex(greater_green[:, block]), n=length, axis=0)
        less_specs.append(less_spec)
        great_specs.append(great_spec)
        cross = less_spec * jnp.conj(great_spec)
        pol_less.append(as_pair(-factor * jnp.fft.ifft(cross, axis=0)[:NE]))
        pol_great.append(as_pair(-factor * jnp.fft.ifft(jnp.conj(cross), axis=0)[:NE]))
    outputs = []
    for kind_list, spec_list in ((pol_less, less_specs), (pol_great, great_specs)):
        stacked = jnp.stack(kind_list, axis=1)
        padded = jnp.pad(stacked, ((0, 0), (1, 1), (0, 0), (0, 0), (0, 0)))
        sigma_list = []
        for block in range(BLOCKS):
            total_re = jnp.zeros((NE, M, M), jnp.float32)
            total_im = jnp.zeros((NE, M, M), jnp.float32)
            for offset in range(3):
                right_re, right_im = congruence(coulomb_blocks[block, offset], padded[:, block + offset])
                total_re = total_re + right_re
                total_im = total_im + right_im
            screen = as_complex(jnp.stack([total_re, total_im], axis=1).astype(jnp.bfloat16))
            screen_spec = jnp.fft.fft(screen, n=length, axis=0)
            sigma = factor * jnp.fft.ifft(spec_list[block] * screen_spec, axis=0)[:NE]
            sigma_list.append(as_pair(sigma))
        outputs.append(jnp.stack(sigma_list, axis=1))
    return (outputs[0], outputs[1])
```

```python
import functools
import math

import numpy as np
import jax
import jax.numpy as jnp
from jax import lax
from jax.experimental import pallas as pl
from jax.experimental.pallas import tpu as pltpu
from jax.sharding import PartitionSpec as P

MESH = pl.DeviceIdType.MESH
BF = jnp.bfloat16
F32 = jnp.float32
PIECES = 32
ROWS = 384
LANES = 128
NE = 64
LENGTH = 2 * NE


def dft_tables():
    f = np.arange(LENGTH)[:, None]
    e = np.arange(NE)[None, :]
    angle = 2.0 * math.pi / LENGTH * (f * e % LENGTH)
    cos, sin = np.cos(angle), np.sin(angle)
    fwd = np.zeros((2, 2, LENGTH, PIECES, 2, 2, 2))
    cs = cos.reshape(LENGTH, PIECES, 2)
    sn = sin.reshape(LENGTH, PIECES, 2)
    for k in range(2):
        fwd[k, 0, :, :, k, :, 0] = cs
        fwd[k, 0, :, :, k, :, 1] = sn
        fwd[k, 1, :, :, k, :, 0] = -sn
        fwd[k, 1, :, :, k, :, 1] = cs
    ct = cs.transpose(1, 2, 0)
    st = sn.transpose(1, 2, 0)
    scale = 1.0 / (math.sqrt(NE) * LENGTH)
    pol = np.zeros((PIECES, 2, 2, 2, 2, LENGTH))
    pol[:, 0, :, 0, 0] = ct
    pol[:, 0, :, 0, 1] = -st
    pol[:, 0, :, 1, 0] = st
    pol[:, 0, :, 1, 1] = ct
    pol[:, 1, :, 0, 0] = ct
    pol[:, 1, :, 0, 1] = st
    pol[:, 1, :, 1, 0] = st
    pol[:, 1, :, 1, 1] = -ct
    sig = np.zeros((PIECES, 2, 2, 2, 2, 2, LENGTH))
    for k in range(2):
        sig[:, k, :, 0, k, 0] = ct
        sig[:, k, :, 0, k, 1] = -st
        sig[:, k, :, 1, k, 0] = st
        sig[:, k, :, 1, k, 1] = ct
    as_bf = lambda a, m, n: jnp.asarray(a.reshape(m, n).astype(np.float32)).astype(BF)
    return (
        as_bf(fwd, 4 * LENGTH, 4 * NE),
        as_bf(-scale * pol, 4 * NE, 2 * LENGTH),
        as_bf(scale * sig, 4 * NE, 4 * LENGTH),
    )


def mirror(t):
    return (t // 8) * 8 + (1 - lax.rem(t // 4, 2)) * 4 + lax.rem(t, 4)


def dot(a, b):
    return jnp.dot(a, b, preferred_element_type=F32)


def kernel(
    lg, gg, cb, fwd_h, pol_h, sig_h, ol, og,
    gin, s0, xb, ps, pr, p3, lf, sc, ss, sx, fs, fr, ob, cc, rr, fwd, pol, sig,
    in_sem, tab_sem, self_sem, send_sem, recv_sem, near_send, near_recv, out_sem,
):
    me = lax.axis_index("energy")
    b = lax.axis_index("blk")
    upper = b >= 2
    my = me // 8
    mz = lax.rem(me // 4, 2)
    mx = lax.rem(me, 4)

    def lag_of(t):
        return jnp.where(upper, mirror(t), t)

    my_lag = lag_of(me)
    inner = jnp.logical_or(b == 1, b == 2)
    core_id = {"energy": me, "blk": b + 1 - 2 * lax.rem(b, 2)}
    cross_id = {"energy": mirror(me), "blk": 3 - b}

    def target(k):
        dz = lax.rem(k, 2)
        dx = lax.rem(k // 2, 4)
        dy = lax.rem(k // 8 + dx, 4)
        return lax.rem(my + dy, 4) * 8 + lax.rem(mz + dz, 2) * 4 + lax.rem(mx + dx, 4)

    def g_copy(c, a):
        src = (lg, gg)[a]
        return pltpu.make_async_copy(
            src.at[:, 0, :, :, pl.ds(LANES * c, LANES)], gin.at[c, a], in_sem.at[c, a]
        )

    for c in range(3):
        for a in range(2):
            g_copy(c, a).start()
    tables = [
        pltpu.make_async_copy(fwd_h, fwd, tab_sem.at[0]),
        pltpu.make_async_copy(pol_h, pol, tab_sem.at[1]),
        pltpu.make_async_copy(sig_h, sig, tab_sem.at[2]),
    ]
    for o in range(3):
        for r in range(2):
            tables.append(
                pltpu.make_async_copy(
                    cb.at[0, o, r], cc.at[o, :, pl.ds(ROWS * r, ROWS)], tab_sem.at[3 + 2 * o + r]
                )
            )
    for copy in tables:
        copy.start()

    barrier = pltpu.get_barrier_semaphore()

    def greet(k, carry):
        pl.semaphore_signal(
            barrier, inc=1, device_id={"energy": target(k), "blk": b}, device_id_type=MESH
        )
        return carry

    lax.fori_loop(1, PIECES, greet, 0)
    pl.semaphore_signal(barrier, inc=1, device_id=core_id, device_id_type=MESH)

    @pl.when(inner)
    def _():
        pl.semaphore_signal(barrier, inc=1, device_id=cross_id, device_id_type=MESH)

    def exchange(stage, part, source, dest, span):
        def go(k, carry):
            t = target(k)
            pltpu.make_async_remote_copy(
                src_ref=source(t), dst_ref=dest(), send_sem=send_sem.at[stage, part],
                recv_sem=recv_sem.at[stage, part], device_id={"energy": t, "blk": b},
                device_id_type=MESH,
            ).start()
            return carry

        lax.fori_loop(1, PIECES, go, 0)
        pltpu.make_async_copy(source(me), dest(), self_sem.at[stage, part]).start()

    def arrived(stage, part, source, dest, span):
        pltpu.make_async_copy(span, span, recv_sem.at[stage, part]).wait()
        pltpu.make_async_copy(source(me), dest(), self_sem.at[stage, part]).wait()

    def sent(stage, part, span):
        pltpu.make_async_copy(span, span, send_sem.at[stage, part]).wait()

    def st0(c):
        return (
            0, c, lambda t: s0.at[c, :, t], lambda: xb.at[c, :, :, me],
            xb.at[c, :, :, pl.ds(0, PIECES - 1)],
        )

    def st1(c):
        return (
            1, c, lambda t: ps.at[c, :, :, lag_of(t)], lambda: pr.at[c, :, me],
            pr.at[c, :, pl.ds(0, PIECES - 1)],
        )

    def st2(r):
        return (
            2, r, lambda t: ss.at[r, t], lambda: sx.at[r, :, :, my_lag],
            sx.at[r, :, :, pl.ds(0, PIECES - 1)],
        )

    def st3(r):
        return (
            3, r, lambda t: fs.at[r, :, :, t], lambda: fr.at[r, me],
            fr.at[r, pl.ds(0, PIECES - 1)],
        )

    for c in range(3):
        for a in range(2):
            g_copy(c, a).wait()

        def pack(i, carry):
            for r in range(3):
                x = gin[c, :, :, :, pl.ds(128 * r + 32 * i, 32), :].reshape(8, 32, LANES)
                s0[c, r, pl.ds(8 * i, 8)] = jnp.swapaxes(x, 0, 1).reshape(8, 4, 8, LANES)
            return carry

        lax.fori_loop(0, 4, pack, 0)
        if c == 0:
            pl.semaphore_wait(barrier, jnp.where(inner, PIECES + 1, PIECES))
        exchange(*st0(c))

    for copy in tables:
        copy.wait()
    for o in range(3):
        cre = cc[o, :, :ROWS].T
        cim = cc[o, :, ROWS:].T
        rr[o, :ROWS, :ROWS] = cre
        rr[o, ROWS:, ROWS:] = cre
        rr[o, ROWS:, :ROWS] = cim
        rr[o, :ROWS, ROWS:] = -cim

    @pl.when(b == 0)
    def _():
        lf[0] = jnp.zeros(lf.shape[1:], BF)

    @pl.when(b == 3)
    def _():
        lf[2] = jnp.zeros(lf.shape[1:], BF)

    def spectrum(x0, x1):
        x = jnp.concatenate([x0.reshape(256, LANES), x1.reshape(256, LANES)], axis=1)
        y = dot(fwd[...], x)
        n = LENGTH
        return y[:n], y[n : 2 * n], y[2 * n : 3 * n], y[3 * n :]

    for c in range(3):
        arrived(*st0(c))

        def correlate(i, carry):
            r, h = i // 2, 2 * lax.rem(i, 2)
            lre, lim, gre, gim = spectrum(xb[c, r, h], xb[c, r, h + 1])
            cross = jnp.concatenate(
                [lre * gre + lim * gim, lim * gre - lre * gim], axis=0
            ).astype(BF)
            p = dot(pol[...], cross).astype(BF)
            ps[c, r, h] = p[:, :LANES].reshape(PIECES, 8, LANES)
            ps[c, r, h + 1] = p[:, LANES:].reshape(PIECES, 8, LANES)
            return carry

        lax.fori_loop(0, 6, correlate, 0)
        exchange(*st1(c))

    def near(c, up):
        slot = 0 if up else 2
        return slot

    def near_copy(c, slot, device):
        return pltpu.make_async_remote_copy(
            src_ref=p3.at[1, c], dst_ref=p3.at[slot, c], send_sem=near_send.at[slot, c],
            recv_sem=near_recv.at[slot, c], device_id=device, device_id_type=MESH,
        )

    even = lax.rem(b, 2) == 0

    def left(o, c):
        def one(q, carry):
            pre = p3[o, c, 2 * q]
            pim = p3[o, c, 2 * q + 1]
            rhs = jnp.concatenate(
                [jnp.concatenate([pre, pim], axis=1), jnp.concatenate([-pim, pre], axis=1)], axis=0
            )
            v = dot(cc[o], rhs).astype(BF)
            for r in range(3):
                lf[o, r, q, :, LANES * c : LANES * c + LANES] = v[128 * r : 128 * r + 128, :LANES]
                lf[o, r, q, :, ROWS + LANES * c : ROWS + LANES * c + LANES] = v[
                    128 * r : 128 * r + 128, LANES:
                ]
            return carry

        lax.fori_loop(0, 4, one, 0)

    for c in range(3):
        arrived(*st1(c))

        def unpack(i, carry):
            for r in range(3):
                x = pr[c, r, pl.ds(8 * i, 8)].reshape(32, 8, LANES)
                p3[1, c, :, pl.ds(128 * r + 32 * i, 32), :] = jnp.swapaxes(x, 0, 1)
            return carry

        lax.fori_loop(0, 4, unpack, 0)

        @pl.when(b < 3)
        def _():
            dev = {"energy": jnp.where(even, me, mirror(me)), "blk": b + 1}
            near_copy(c, 0, dev).start()

        @pl.when(b > 0)
        def _():
            dev = {"energy": jnp.where(even, mirror(me), me), "blk": b - 1}
            near_copy(c, 2, dev).start()

        left(1, c)

    for c in range(3):
        @pl.when(b > 0)
        def _():
            near_copy(c, 0, core_id).wait_recv()
            left(0, c)

        @pl.when(b < 3)
        def _():
            near_copy(c, 2, core_id).wait_recv()
            left(2, c)

    def right(r, carry):
        for n in range(3):
            v = sum(
                dot(lf[o, r].reshape(512, 2 * ROWS), rr[o, :, 256 * n : 256 * n + 256])
                for o in range(3)
            ).astype(BF)
            for h in range(2):
                part, c = divmod(2 * n + h, 3)
                for q in range(4):
                    sc[c, 2 * q + part] = v[128 * q : 128 * q + 128, LANES * h : LANES * h + LANES]

        def pack(i, carry):
            for c in range(3):
                x = sc[c, :, pl.ds(32 * i, 32), :]
                ss[r, pl.ds(8 * i, 8), :, c] = jnp.swapaxes(x, 0, 1).reshape(8, 4, 8, LANES)
            return carry

        lax.fori_loop(0, 4, pack, 0)
        exchange(*st2(r))
        return carry

    lax.fori_loop(0, 3, right, 0)

    def convolve(r, carry):
        arrived(*st2(r))

        def one(i, carry):
            u = 2 * i
            xs, ws = [], []
            for j in range(2):
                row, c = (u + j) // 3, lax.rem(u + j, 3)
                xs.append(xb[c, r, row])
                ws.append(sx[r, row, c])
            lre, lim, gre, gim = spectrum(*xs)
            a, d, e, g = spectrum(*ws)
            m = jnp.concatenate(
                [lre * a - lim * d, lre * d + lim * a, gre * e - gim * g, gre * g + gim * e], axis=0
            ).astype(BF)
            v = dot(sig[...], m).astype(BF)
            for j in range(2):
                row, c = (u + j) // 3, lax.rem(u + j, 3)
                fs[r, row, c] = v[:, LANES * j : LANES * j + LANES].reshape(PIECES, 8, LANES)
            return carry

        lax.fori_loop(0, 6, one, 0)
        exchange(*st3(r))
        return carry

    lax.fori_loop(0, 3, convolve, 0)

    def out_copy(r, a):
        dst = (ol, og)[a]
        return pltpu.make_async_copy(
            ob.at[r, a], dst.at[:, 0, :, pl.ds(128 * r, 128), :], out_sem.at[r, a]
        )

    def finish(r, carry):
        arrived(*st3(r))

        def unpack(i, carry):
            for c in range(3):
                x = fr[r, pl.ds(8 * i, 8), :, c].reshape(32, 8, LANES)
                ob[r, :, :, :, pl.ds(32 * i, 32), LANES * c : LANES * c + LANES] = jnp.swapaxes(
                    x, 0, 1
                ).reshape(2, 2, 2, 32, LANES)
            return carry

        lax.fori_loop(0, 4, unpack, 0)
        for a in range(2):
            out_copy(r, a).start()
        return carry

    lax.fori_loop(0, 3, finish, 0)

    for r in range(3):
        for st in (st0, st1, st2, st3):
            stage, part, _, _, span = st(r)
            sent(stage, part, span)

        @pl.when(b < 3)
        def _():
            near_copy(r, 0, core_id).wait_send()

        @pl.when(b > 0)
        def _():
            near_copy(r, 2, core_id).wait_send()

        for a in range(2):
            out_copy(r, a).wait()


def local(lesser_green, greater_green, coulomb_blocks):
    fwd, pol, sig = dft_tables()
    any_spec = pl.BlockSpec(memory_space=pl.ANY)
    out = jax.ShapeDtypeStruct(lesser_green.shape, BF)
    tile = (8, LANES)
    dma = pltpu.SemaphoreType.DMA
    return pl.pallas_call(
        kernel,
        out_shape=(out, out),
        in_specs=[any_spec] * 6,
        out_specs=(any_spec, any_spec),
        scratch_shapes=[
            pltpu.VMEM((3, 2, 2, 2, ROWS, LANES), BF),
            pltpu.VMEM((3, 3, PIECES, 4) + tile, BF),
            pltpu.VMEM((3, 3, 4, PIECES) + tile, BF),
            pltpu.VMEM((3, 3, 4, PIECES) + tile, BF),
            pltpu.VMEM((3, 3, PIECES, 4) + tile, BF),
            pltpu.VMEM((3, 3, 8, ROWS, LANES), BF),
            pltpu.VMEM((3, 3, 4, 128, 2 * ROWS), BF),
            pltpu.VMEM((3, 8, 128, LANES), BF),
            pltpu.VMEM((3, PIECES, 4, 3) + tile, BF),
            pltpu.VMEM((3, 4, 3, PIECES) + tile, BF),
            pltpu.VMEM((3, 4, 3, PIECES) + tile, BF),
            pltpu.VMEM((3, PIECES, 4, 3) + tile, BF),
            pltpu.VMEM((3, 2, 2, 2, 128, ROWS), BF),
            pltpu.VMEM((3, ROWS, 2 * ROWS), BF),
            pltpu.VMEM((3, 2 * ROWS, 2 * ROWS), BF),
            pltpu.VMEM((4 * LENGTH, 4 * NE), BF),
            pltpu.VMEM((4 * NE, 2 * LENGTH), BF),
            pltpu.VMEM((4 * NE, 4 * LENGTH), BF),
            dma((3, 2)), dma((9,)), dma((4, 3)), dma((4, 3)), dma((4, 3)), dma((3, 3)), dma((3, 3)),
            dma((3, 2)),
        ],
        compiler_params=pltpu.CompilerParams(
            collective_id=0, has_side_effects=True, vmem_limit_bytes=66_000_000
        ),
        name="gw",
    )(lesser_green, greater_green, coulomb_blocks, fwd, pol, sig)


def solution(mesh):
    return jax.shard_map(
        local,
        mesh=mesh,
        in_specs=(
            P("energy", "blk", None, None, None),
            P("energy", "blk", None, None, None),
            P("blk", None, None, None, None),
        ),
        out_specs=(P("energy", "blk", None, None, None), P("energy", "blk", None, None, None)),
        check_vma=False,
    )
```

```python
import functools
import math

import numpy as np
import jax
import jax.numpy as jnp
from jax import lax
from jax.experimental import pallas as pl
from jax.experimental.pallas import tpu as pltpu
from jax.sharding import PartitionSpec as P

MESH = pl.DeviceIdType.MESH
BF = jnp.bfloat16
F32 = jnp.float32
PIECES = 32
ROWS = 384
LANES = 128
NE = 64
LENGTH = 2 * NE


def dft_tables():
    f = np.arange(LENGTH)[:, None]
    e = np.arange(NE)[None, :]
    angle = 2.0 * math.pi / LENGTH * (f * e % LENGTH)
    cos, sin = np.cos(angle), np.sin(angle)
    fwd = np.zeros((2, 2, LENGTH, PIECES, 2, 2, 2))
    cs = cos.reshape(LENGTH, PIECES, 2)
    sn = sin.reshape(LENGTH, PIECES, 2)
    for k in range(2):
        fwd[k, 0, :, :, k, :, 0] = cs
        fwd[k, 0, :, :, k, :, 1] = sn
        fwd[k, 1, :, :, k, :, 0] = -sn
        fwd[k, 1, :, :, k, :, 1] = cs
    ct = cs.transpose(1, 2, 0)
    st = sn.transpose(1, 2, 0)
    scale = 1.0 / (math.sqrt(NE) * LENGTH)
    pol = np.zeros((2, PIECES, 2, 2, 2, 2, 2, LENGTH))
    for h in range(2):
        pol[0, :, h, :, 0, h, 0] = ct
        pol[0, :, h, :, 0, h, 1] = -st
        pol[0, :, h, :, 1, h, 0] = st
        pol[0, :, h, :, 1, h, 1] = ct
        pol[1, :, h, :, 0, h, 0] = ct
        pol[1, :, h, :, 0, h, 1] = st
        pol[1, :, h, :, 1, h, 0] = st
        pol[1, :, h, :, 1, h, 1] = -ct
    sig = np.zeros((PIECES, 2, 2, 2, 2, 2, LENGTH))
    for k in range(2):
        sig[:, k, :, 0, k, 0] = ct
        sig[:, k, :, 0, k, 1] = -st
        sig[:, k, :, 1, k, 0] = st
        sig[:, k, :, 1, k, 1] = ct
    as_bf = lambda a, m, n: jnp.asarray(a.reshape(m, n).astype(np.float32)).astype(BF)
    return (
        as_bf(fwd, 4 * LENGTH, 4 * NE),
        as_bf(-scale * pol, 8 * NE, 4 * LENGTH),
        as_bf(scale * sig, 4 * NE, 4 * LENGTH),
    )


def mirror(t):
    return (t // 8) * 8 + (1 - lax.rem(t // 4, 2)) * 4 + lax.rem(t, 4)


def dot(a, b):
    return jnp.dot(a, b, preferred_element_type=F32)


def kernel(
    lg, gg, cb, fwd_h, pol_h, sig_h, ol, og,
    gin, s0, xb, ps, pr, p3, lf, sc, ss, sx, fs, fr, ob, cc, rr, fwd, pol, sig,
    in_sem, tab_sem, self_sem, send_sem, recv_sem, near_send, near_recv, out_sem,
):
    me = lax.axis_index("energy")
    b = lax.axis_index("blk")
    upper = b >= 2
    even = lax.rem(b, 2) == 0
    my = me // 8
    mz = lax.rem(me // 4, 2)
    mx = lax.rem(me, 4)

    def lag_of(t):
        return jnp.where(upper, mirror(t), t)

    my_lag = lag_of(me)
    inner = jnp.logical_or(b == 1, b == 2)
    core_id = {"energy": me, "blk": b + 1 - 2 * lax.rem(b, 2)}
    cross_id = {"energy": mirror(me), "blk": 3 - b}

    def target(k):
        dz = lax.rem(k, 2)
        dx = lax.rem(k // 2, 4)
        dy = lax.rem(k // 8 + dx, 4)
        return lax.rem(my + dy, 4) * 8 + lax.rem(mz + dz, 2) * 4 + lax.rem(mx + dx, 4)

    def g_copy(c, a):
        src = (lg, gg)[a]
        return pltpu.make_async_copy(
            src.at[:, 0, :, :, pl.ds(LANES * c, LANES)], gin.at[c, a], in_sem.at[c, a]
        )

    for c in range(3):
        for a in range(2):
            g_copy(c, a).start()
    tables = [
        pltpu.make_async_copy(fwd_h, fwd, tab_sem.at[0]),
        pltpu.make_async_copy(pol_h, pol, tab_sem.at[1]),
        pltpu.make_async_copy(sig_h, sig, tab_sem.at[2]),
    ]
    for o in range(3):
        for r in range(2):
            tables.append(
                pltpu.make_async_copy(
                    cb.at[0, o, r], cc.at[o, :, pl.ds(ROWS * r, ROWS)], tab_sem.at[3 + 2 * o + r]
                )
            )
    for copy in tables:
        copy.start()

    barrier = pltpu.get_barrier_semaphore()

    def greet(k, carry):
        pl.semaphore_signal(
            barrier, inc=1, device_id={"energy": target(k), "blk": b}, device_id_type=MESH
        )
        return carry

    lax.fori_loop(1, PIECES, greet, 0)
    pl.semaphore_signal(barrier, inc=1, device_id=core_id, device_id_type=MESH)

    @pl.when(inner)
    def _():
        pl.semaphore_signal(barrier, inc=1, device_id=cross_id, device_id_type=MESH)

    def exchange(stage, part, source, dest, span):
        def go(k, carry):
            t = target(k)
            pltpu.make_async_remote_copy(
                src_ref=source(t), dst_ref=dest(), send_sem=send_sem.at[stage, part],
                recv_sem=recv_sem.at[stage, part], device_id={"energy": t, "blk": b},
                device_id_type=MESH,
            ).start()
            return carry

        lax.fori_loop(1, PIECES, go, 0)
        pltpu.make_async_copy(source(me), dest(), self_sem.at[stage, part]).start()

    def arrived(stage, part, source, dest, span):
        pltpu.make_async_copy(span, span, recv_sem.at[stage, part]).wait()
        pltpu.make_async_copy(source(me), dest(), self_sem.at[stage, part]).wait()

    def sent(stage, part, span):
        pltpu.make_async_copy(span, span, send_sem.at[stage, part]).wait()

    others = pl.ds(0, PIECES - 1)

    def st0(c):
        return (
            0, c, lambda t: s0.at[c, :, :, t], lambda: xb.at[c, :, :, :, me],
            xb.at[c, :, :, :, others],
        )

    def st1(k, c):
        return (
            1, 3 * k + c, lambda t: ps.at[k, c, :, :, lag_of(t)], lambda: pr.at[k, c, :, me],
            pr.at[k, c, :, others],
        )

    def st2(k, r):
        return (
            2, 3 * k + r, lambda t: ss.at[k, r, t], lambda: sx.at[k, r, :, :, my_lag],
            sx.at[k, r, :, :, others],
        )

    def st3(k, r):
        return (
            3, 3 * k + r, lambda t: fs.at[k, r, :, :, t], lambda: fr.at[k, r, me],
            fr.at[k, r, others],
        )

    for c in range(3):
        for a in range(2):
            g_copy(c, a).wait()

        def pack(i, carry):
            r, h = i // 2, lax.rem(i, 2)
            for j in range(2):
                x = gin[c, :, :, :, pl.ds(64 * i + 32 * j, 32), :].reshape(8, 32, LANES)
                s0[c, r, h, 16 * j : 16 * j + 16] = jnp.swapaxes(x, 0, 1).reshape(16, 2, 8, LANES)
            return carry

        lax.fori_loop(0, 6, pack, 0)
        if c == 0:
            pl.semaphore_wait(barrier, jnp.where(inner, PIECES + 1, PIECES))
        exchange(*st0(c))

    for copy in tables:
        copy.wait()
    for o in range(3):
        cre = cc[o, :, :ROWS].T
        cim = cc[o, :, ROWS:].T
        rr[o, :ROWS, :ROWS] = cre
        rr[o, ROWS:, ROWS:] = cre
        rr[o, ROWS:, :ROWS] = cim
        rr[o, :ROWS, ROWS:] = -cim

    @pl.when(b == 0)
    def _():
        lf[:, :, :, :, : 2 * ROWS] = jnp.zeros(lf.shape[:4] + (2 * ROWS,), BF)

    @pl.when(b == 3)
    def _():
        lf[:, :, :, :, 4 * ROWS :] = jnp.zeros(lf.shape[:4] + (2 * ROWS,), BF)

    n = LENGTH

    def side(x0, x1):
        return jnp.concatenate([x0.reshape(256, LANES), x1.reshape(256, LANES)], axis=1)

    def polarize(c, carry):
        arrived(*st0(c))

        def one(r, carry):
            cross = []
            for h in range(2):
                y = dot(fwd[...], side(xb[c, r, h, 0], xb[c, r, h, 1]))
                lre, lim, gre, gim = y[:n], y[n : 2 * n], y[2 * n : 3 * n], y[3 * n :]
                cross += [lre * gre + lim * gim, lim * gre - lre * gim]
            p = dot(pol[...], jnp.concatenate(cross, axis=0).astype(BF)).astype(BF)
            for k in range(2):
                for i in range(2):
                    ps[k, c, r, i] = p[
                        256 * k : 256 * k + 256, LANES * i : LANES * i + LANES
                    ].reshape(PIECES, 8, LANES)
            return carry

        lax.fori_loop(0, 3, one, 0, unroll=True)
        exchange(*st1(0, c))
        return carry

    lax.fori_loop(0, 3, polarize, 0)

    def second(c, carry):
        exchange(*st1(1, c))
        return carry

    lax.fori_loop(0, 3, second, 0)

    def near_copy(k, c, slot, device):
        return pltpu.make_async_remote_copy(
            src_ref=p3.at[k, 1, c], dst_ref=p3.at[k, slot, c], send_sem=near_send.at[k, slot, c],
            recv_sem=near_recv.at[k, slot, c], device_id=device, device_id_type=MESH,
        )

    def left(k, o, c):
        for q in range(2):
            pre = p3[k, o, c, 2 * q].reshape(ROWS, LANES)
            pim = p3[k, o, c, 2 * q + 1].reshape(ROWS, LANES)
            rhs = jnp.concatenate(
                [jnp.concatenate([pre, pim], axis=1), jnp.concatenate([-pim, pre], axis=1)], axis=0
            )
            v = dot(cc[o], rhs).astype(BF)
            for r in range(3):
                for p in range(2):
                    at = 2 * ROWS * o + ROWS * p + LANES * c
                    lf[k, r, q, :, at : at + LANES] = v[
                        128 * r : 128 * r + 128, LANES * p : LANES * p + LANES
                    ]

    def congruence(k, carry):
        for c in range(3):
            arrived(*st1(k, c))
            for r in range(3):
                for j in range(2):
                    x = pr[k, c, r, 16 * j : 16 * j + 16].reshape(32, 8, LANES)
                    x = jnp.swapaxes(x, 0, 1)
                    for h in range(2):
                        p3[k, 1, c, :, r, h, 32 * j : 32 * j + 32, :] = x[4 * h : 4 * h + 4]

            @pl.when(b < 3)
            def _():
                dev = {"energy": jnp.where(even, me, mirror(me)), "blk": b + 1}
                near_copy(k, c, 0, dev).start()

            @pl.when(b > 0)
            def _():
                dev = {"energy": jnp.where(even, mirror(me), me), "blk": b - 1}
                near_copy(k, c, 2, dev).start()

            left(k, 1, c)

        for c in range(3):
            @pl.when(b > 0)
            def _():
                near_copy(k, c, 0, core_id).wait_recv()
                left(k, 0, c)

            @pl.when(b < 3)
            def _():
                near_copy(k, c, 2, core_id).wait_recv()
                left(k, 2, c)

        for m in range(3):
            v = dot(
                lf[k].reshape(6 * 128, 6 * ROWS),
                rr[:, :, 256 * m : 256 * m + 256].reshape(6 * ROWS, 256),
            ).astype(BF)
            for h in range(2):
                part, c = divmod(2 * m + h, 3)
                for r in range(3):
                    for q in range(2):
                        at = 256 * r + 128 * q
                        sc[c, 2 * q + part, r] = v[
                            at : at + 128, LANES * h : LANES * h + LANES
                        ].reshape(2, 64, LANES)

        def send(r, carry):
            for c in range(3):
                for j in range(2):
                    x = jnp.concatenate(
                        [sc[c, :, r, h, 32 * j : 32 * j + 32, :] for h in range(2)], axis=0
                    )
                    ss[k, r, 16 * j : 16 * j + 16, :, c] = jnp.swapaxes(x, 0, 1).reshape(
                        16, 2, 8, LANES
                    )
            exchange(*st2(k, r))
            return carry

        lax.fori_loop(0, 3, send, 0)
        return carry

    lax.fori_loop(0, 2, congruence, 0)

    def convolve(m, carry):
        k, r = m // 3, lax.rem(m, 3)
        arrived(*st2(k, r))
        half = fwd[pl.ds(pl.multiple_of(256 * k, 256), 256), :]

        def one(c, carry):
            w = dot(fwd[...], side(sx[k, r, 0, c], sx[k, r, 1, c]))
            prod = []
            for h in range(2):
                g = dot(half, side(xb[c, r, h, 0], xb[c, r, h, 1]))
                gre, gim = g[:n], g[n:]
                wre, wim = w[2 * n * h : 2 * n * h + n], w[2 * n * h + n : 2 * n * h + 2 * n]
                prod += [gre * wre - gim * wim, gre * wim + gim * wre]
            v = dot(sig[...], jnp.concatenate(prod, axis=0).astype(BF)).astype(BF)
            for i in range(2):
                fs[k, r, i, c] = v[:, LANES * i : LANES * i + LANES].reshape(PIECES, 8, LANES)
            return carry

        lax.fori_loop(0, 3, one, 0, unroll=True)
        exchange(*st3(k, r))
        return carry

    lax.fori_loop(0, 6, convolve, 0)

    def out_copy(k, r):
        dst = (ol, og)[k]
        return pltpu.make_async_copy(
            ob.at[k, r], dst.at[:, 0, :, pl.ds(128 * r, 128), :], out_sem.at[k, r]
        )

    for k in range(2):

        def finish(r, carry):
            arrived(*st3(k, r))
            for c in range(3):
                for j in range(2):
                    x = fr[k, r, 16 * j : 16 * j + 16, :, c].reshape(32, 8, LANES)
                    x = jnp.swapaxes(x, 0, 1)
                    for h in range(2):
                        at = 64 * h + 32 * j
                        ob[k, r, :, :, at : at + 32, LANES * c : LANES * c + LANES] = x[
                            4 * h : 4 * h + 4
                        ].reshape(2, 2, 32, LANES)
            out_copy(k, r).start()
            return carry

        lax.fori_loop(0, 3, finish, 0)

    for r in range(3):
        sent(*[st0(r)[i] for i in (0, 1, 4)])

    def drain(m, carry):
        k, r = m // 3, lax.rem(m, 3)
        for st in (st1, st2, st3):
            sent(*[st(k, r)[i] for i in (0, 1, 4)])

        @pl.when(b < 3)
        def _():
            near_copy(k, r, 0, core_id).wait_send()

        @pl.when(b > 0)
        def _():
            near_copy(k, r, 2, core_id).wait_send()

        return carry

    lax.fori_loop(0, 6, drain, 0)
    for k in range(2):
        for r in range(3):
            out_copy(k, r).wait()


def local(lesser_green, greater_green, coulomb_blocks):
    fwd, pol, sig = dft_tables()
    any_spec = pl.BlockSpec(memory_space=pl.ANY)
    out = jax.ShapeDtypeStruct(lesser_green.shape, BF)
    tile = (8, LANES)
    dma = pltpu.SemaphoreType.DMA
    return pl.pallas_call(
        kernel,
        out_shape=(out, out),
        in_specs=[any_spec] * 6,
        out_specs=(any_spec, any_spec),
        scratch_shapes=[
            pltpu.VMEM((3, 2, 2, 2, ROWS, LANES), BF),
            pltpu.VMEM((3, 3, 2, PIECES, 2) + tile, BF),
            pltpu.VMEM((3, 3, 2, 2, PIECES) + tile, BF),
            pltpu.VMEM((2, 3, 3, 2, PIECES) + tile, BF),
            pltpu.VMEM((2, 3, 3, PIECES, 2) + tile, BF),
            pltpu.VMEM((2, 3, 3, 4, 3, 2, 64, LANES), BF),
            pltpu.VMEM((2, 3, 2, 128, 6 * ROWS), BF),
            pltpu.VMEM((3, 4, 3, 2, 64, LANES), BF),
            pltpu.VMEM((2, 3, PIECES, 2, 3) + tile, BF),
            pltpu.VMEM((2, 3, 2, 3, PIECES) + tile, BF),
            pltpu.VMEM((2, 3, 2, 3, PIECES) + tile, BF),
            pltpu.VMEM((2, 3, PIECES, 2, 3) + tile, BF),
            pltpu.VMEM((2, 3, 2, 2, 128, ROWS), BF),
            pltpu.VMEM((3, ROWS, 2 * ROWS), BF),
            pltpu.VMEM((3, 2 * ROWS, 2 * ROWS), BF),
            pltpu.VMEM((4 * LENGTH, 4 * NE), BF),
            pltpu.VMEM((8 * NE, 4 * LENGTH), BF),
            pltpu.VMEM((4 * NE, 4 * LENGTH), BF),
            dma((3, 2)), dma((9,)), dma((4, 6)), dma((4, 6)), dma((4, 6)), dma((2, 3, 3)),
            dma((2, 3, 3)), dma((2, 3)),
        ],
        compiler_params=pltpu.CompilerParams(
            collective_id=0, has_side_effects=True, vmem_limit_bytes=66_000_000
        ),
        name="gw",
    )(lesser_green, greater_green, coulomb_blocks, fwd, pol, sig)


def solution(mesh):
    return jax.shard_map(
        local,
        mesh=mesh,
        in_specs=(
            P("energy", "blk", None, None, None),
            P("energy", "blk", None, None, None),
            P("blk", None, None, None, None),
        ),
        out_specs=(P("energy", "blk", None, None, None), P("energy", "blk", None, None, None)),
        check_vma=False,
    )
```

```python
import functools
import math

import numpy as np
import jax
import jax.numpy as jnp
from jax import lax
from jax.experimental import pallas as pl
from jax.experimental.pallas import tpu as pltpu
from jax.sharding import PartitionSpec as P

MESH = pl.DeviceIdType.MESH
BF = jnp.bfloat16
F32 = jnp.float32
PIECES = 32
ROWS = 384
LANES = 128
NE = 64
LENGTH = 2 * NE


def dft_tables():
    f = np.arange(LENGTH)[:, None]
    e = np.arange(NE)[None, :]
    angle = 2.0 * math.pi / LENGTH * (f * e % LENGTH)
    cos, sin = np.cos(angle), np.sin(angle)
    fwd = np.zeros((2, 2, LENGTH, PIECES, 2, 2, 2))
    cs = cos.reshape(LENGTH, PIECES, 2)
    sn = sin.reshape(LENGTH, PIECES, 2)
    for k in range(2):
        fwd[k, 0, :, :, k, :, 0] = cs
        fwd[k, 0, :, :, k, :, 1] = sn
        fwd[k, 1, :, :, k, :, 0] = -sn
        fwd[k, 1, :, :, k, :, 1] = cs
    ct = cs.transpose(1, 2, 0)
    st = sn.transpose(1, 2, 0)
    scale = 1.0 / (math.sqrt(NE) * LENGTH)
    pol = np.zeros((2, PIECES, 2, 2, 2, 2, 2, LENGTH))
    for h in range(2):
        pol[0, :, h, :, 0, h, 0] = ct
        pol[0, :, h, :, 0, h, 1] = -st
        pol[0, :, h, :, 1, h, 0] = st
        pol[0, :, h, :, 1, h, 1] = ct
        pol[1, :, h, :, 0, h, 0] = ct
        pol[1, :, h, :, 0, h, 1] = st
        pol[1, :, h, :, 1, h, 0] = st
        pol[1, :, h, :, 1, h, 1] = -ct
    sig = np.zeros((PIECES, 2, 2, 2, 2, 2, LENGTH))
    for k in range(2):
        sig[:, k, :, 0, k, 0] = ct
        sig[:, k, :, 0, k, 1] = -st
        sig[:, k, :, 1, k, 0] = st
        sig[:, k, :, 1, k, 1] = ct
    as_bf = lambda a, m, n: jnp.asarray(a.reshape(m, n).astype(np.float32)).astype(BF)
    return (
        as_bf(fwd, 4 * LENGTH, 4 * NE),
        as_bf(-scale * pol, 8 * NE, 4 * LENGTH),
        as_bf(scale * sig, 4 * NE, 4 * LENGTH),
    )


def mirror(t):
    return (t // 8) * 8 + (1 - lax.rem(t // 4, 2)) * 4 + lax.rem(t, 4)


def dot(a, b):
    return jnp.dot(a, b, preferred_element_type=F32)


def kernel(
    lg, gg, cb, fwd_h, pol_h, sig_h, ol, og,
    gin, s0, xb, ps, pr, p3, lf, acc, sc, ss, sx, fs, fr, ob, cc, rr, fwd, pol, sig,
    in_sem, tab_sem, self_sem, send_sem, recv_sem, near_send, near_recv, out_sem,
):
    me = lax.axis_index("energy")
    b = lax.axis_index("blk")
    upper = b >= 2
    even = lax.rem(b, 2) == 0
    my = me // 8
    mz = lax.rem(me // 4, 2)
    mx = lax.rem(me, 4)
    inner = jnp.logical_or(b == 1, b == 2)
    core_id = {"energy": me, "blk": b + 1 - 2 * lax.rem(b, 2)}
    cross_id = {"energy": mirror(me), "blk": 3 - b}
    core_o = jnp.where(even, 2, 0)
    offsets = (1, core_o, 2 - core_o)

    ys = [8 * lax.rem(my + d, 4) for d in range(4)]
    xs = [lax.rem(mx + d, 4) for d in range(4)]
    zs = [4 * mz, 4 - 4 * mz]
    lag_zs = [jnp.where(upper, 4 - z, z) for z in zs]
    my_lag = 8 * my + lag_zs[0] + mx
    peers = []
    for k in range(PIECES):
        dz, dx = k % 2, k // 2 % 4
        dy = (k // 8 + dx) % 4
        peers.append((ys[dy] + zs[dz] + xs[dx], ys[dy] + lag_zs[dz] + xs[dx]))

    barrier = pltpu.get_barrier_semaphore()
    for t, _ in reversed(peers[1:]):
        pl.semaphore_signal(
            barrier, inc=1, device_id={"energy": t, "blk": b}, device_id_type=MESH
        )
    pl.semaphore_signal(barrier, inc=1, device_id=core_id, device_id_type=MESH)

    @pl.when(inner)
    def _():
        pl.semaphore_signal(barrier, inc=1, device_id=cross_id, device_id_type=MESH)

    def g_copy(c, a):
        src = (lg, gg)[a]
        return pltpu.make_async_copy(
            src.at[:, 0, :, :, pl.ds(LANES * c, LANES)], gin.at[c, a], in_sem.at[c, a]
        )

    for a in range(2):
        g_copy(0, a).start()
    tables = [
        pltpu.make_async_copy(fwd_h, fwd, tab_sem.at[0]),
        pltpu.make_async_copy(pol_h, pol, tab_sem.at[1]),
        pltpu.make_async_copy(sig_h, sig, tab_sem.at[2]),
    ]
    for o in range(3):
        for r in range(2):
            tables.append(
                pltpu.make_async_copy(
                    cb.at[0, offsets[o], r],
                    cc.at[o, :, pl.ds(ROWS * r, ROWS)],
                    tab_sem.at[3 + 2 * o + r],
                )
            )

    def exchange(stage, part, source, dest, span):
        for t, lag in peers[1:]:
            pltpu.make_async_remote_copy(
                src_ref=source(t, lag), dst_ref=dest(), send_sem=send_sem.at[stage, part],
                recv_sem=recv_sem.at[stage, part], device_id={"energy": t, "blk": b},
                device_id_type=MESH,
            ).start()
        pltpu.make_async_copy(source(me, my_lag), dest(), self_sem.at[stage, part]).start()

    def arrived(stage, part, source, dest, span):
        pltpu.make_async_copy(span, span, recv_sem.at[stage, part]).wait()
        pltpu.make_async_copy(source(me, my_lag), dest(), self_sem.at[stage, part]).wait()

    def sent(stage, part, span):
        pltpu.make_async_copy(span, span, send_sem.at[stage, part]).wait()

    others = pl.ds(0, PIECES - 1)

    def st0(c):
        return (
            0, c, lambda t, lag: s0.at[c, :, :, t], lambda: xb.at[c, :, :, :, me],
            xb.at[c, :, :, :, others],
        )

    def st1(k, c):
        return (
            1, 3 * k + c, lambda t, lag: ps.at[k, c, :, :, lag], lambda: pr.at[k, c, :, me],
            pr.at[k, c, :, others],
        )

    def st2(k, r):
        return (
            2, 3 * k + r, lambda t, lag: ss.at[k, r, t], lambda: sx.at[k, r, :, :, my_lag],
            sx.at[k, r, :, :, others],
        )

    def st3(k, r):
        return (
            3, 3 * k + r, lambda t, lag: fs.at[k, r, :, :, t], lambda: fr.at[k, r, me],
            fr.at[k, r, others],
        )

    for c in range(3):
        for a in range(2):
            g_copy(c, a).wait()
        if c == 0:
            for d in range(1, 3):
                for a in range(2):
                    g_copy(d, a).start()

        def pack(i, carry):
            r, h = i // 2, lax.rem(i, 2)
            for j in range(2):
                x = gin[c, :, :, :, pl.ds(64 * i + 32 * j, 32), :].reshape(8, 32, LANES)
                s0[c, r, h, 16 * j : 16 * j + 16] = jnp.swapaxes(x, 0, 1).reshape(16, 2, 8, LANES)
            return carry

        lax.fori_loop(0, 6, pack, 0)
        if c == 0:
            pl.semaphore_wait(barrier, jnp.where(inner, PIECES + 1, PIECES))
        exchange(*st0(c))

    for copy in tables:
        copy.start()
    for copy in tables:
        copy.wait()
    for o in range(3):
        cre = cc[o, :, :ROWS].T
        cim = cc[o, :, ROWS:].T
        rr[o, :ROWS, :ROWS] = cre
        rr[o, ROWS:, ROWS:] = cre
        rr[o, ROWS:, :ROWS] = cim
        rr[o, :ROWS, ROWS:] = -cim

    n = LENGTH

    def side(x0, x1):
        return jnp.concatenate([x0.reshape(256, LANES), x1.reshape(256, LANES)], axis=1)

    def polarize(c, carry):
        arrived(*st0(c))

        def one(r, carry):
            cross = []
            for h in range(2):
                y = dot(fwd[...], side(xb[c, r, h, 0], xb[c, r, h, 1]))
                lre, lim, gre, gim = y[:n], y[n : 2 * n], y[2 * n : 3 * n], y[3 * n :]
                cross += [lre * gre + lim * gim, lim * gre - lre * gim]
            p = dot(pol[...], jnp.concatenate(cross, axis=0).astype(BF)).astype(BF)
            for k in range(2):
                for i in range(2):
                    ps[k, c, r, i] = p[
                        256 * k : 256 * k + 256, LANES * i : LANES * i + LANES
                    ].reshape(PIECES, 8, LANES)
            return carry

        lax.fori_loop(0, 3, one, 0, unroll=True)
        exchange(*st1(0, c))
        return carry

    lax.fori_loop(0, 3, polarize, 0)

    exchange(*st1(1, 0))

    def near_copy(k, c, slot):
        return pltpu.make_async_remote_copy(
            src_ref=p3.at[k, 0, c], dst_ref=p3.at[k, slot, c], send_sem=near_send.at[k, slot, c],
            recv_sem=near_recv.at[k, slot, c], device_id=core_id if slot == 1 else cross_id,
            device_id_type=MESH,
        )

    def unpack(k, c):
        arrived(*st1(k, c))
        for r in range(3):
            for j in range(2):
                x = pr[k, c, r, 16 * j : 16 * j + 16].reshape(32, 8, LANES)
                x = jnp.swapaxes(x, 0, 1)
                for h in range(2):
                    p3[k, 0, c, :, r, h, 32 * j : 32 * j + 32, :] = x[4 * h : 4 * h + 4]

        @pl.when(inner)
        def _():
            near_copy(k, c, 2).start()

        near_copy(k, c, 1).start()

    def left(k, o, c):
        for q in range(2):
            pre = p3[k, o, c, 2 * q].reshape(ROWS, LANES)
            pim = p3[k, o, c, 2 * q + 1].reshape(ROWS, LANES)
            rhs = jnp.concatenate(
                [jnp.concatenate([pre, pim], axis=1), jnp.concatenate([-pim, pre], axis=1)], axis=0
            )
            v = dot(cc[o], rhs).astype(BF)
            for p in range(2):
                at = 2 * ROWS * o + ROWS * p + LANES * c
                for r in range(3):
                    lf[k, r, q, :, at : at + LANES] = v[
                        128 * r : 128 * r + 128, LANES * p : LANES * p + LANES
                    ]

    def beside(k, c):
        near_copy(k, c, 1).wait_recv()
        left(k, 1, c)

    def across(k, c):
        @pl.when(inner)
        def _():
            near_copy(k, c, 2).wait_recv()
            left(k, 2, c)

    def right_near(k):
        for m in range(3):
            acc[:, 256 * m : 256 * m + 256] = dot(
                lf[k, :, :, :, : 4 * ROWS].reshape(6 * 128, 4 * ROWS),
                rr[:2, :, 256 * m : 256 * m + 256].reshape(4 * ROWS, 256),
            )

    def right_far(k):
        def emit(m, v):
            v = v.astype(BF)
            for h in range(2):
                part, c = divmod(2 * m + h, 3)
                for r in range(3):
                    for q in range(2):
                        at = 256 * r + 128 * q
                        sc[c, 2 * q + part, r] = v[
                            at : at + 128, LANES * h : LANES * h + LANES
                        ].reshape(2, 64, LANES)

        @pl.when(inner)
        def _():
            for m in range(3):
                emit(
                    m,
                    acc[:, 256 * m : 256 * m + 256]
                    + dot(
                        lf[k, :, :, :, 4 * ROWS :].reshape(6 * 128, 2 * ROWS),
                        rr[2, :, 256 * m : 256 * m + 256],
                    ),
                )

        @pl.when(jnp.logical_not(inner))
        def _():
            for m in range(3):
                emit(m, acc[:, 256 * m : 256 * m + 256])

    def send(k, r):
        for c in range(3):
            for j in range(2):
                x = jnp.concatenate(
                    [sc[c, :, r, h, 32 * j : 32 * j + 32, :] for h in range(2)], axis=0
                )
                ss[k, r, 16 * j : 16 * j + 16, :, c] = jnp.swapaxes(x, 0, 1).reshape(
                    16, 2, 8, LANES
                )
        exchange(*st2(k, r))

    unpack(0, 0)
    exchange(*st1(1, 1))
    unpack(0, 1)
    exchange(*st1(1, 2))
    left(0, 0, 0)
    left(0, 0, 1)
    beside(0, 0)
    unpack(0, 2)
    left(0, 0, 2)
    beside(0, 1)
    beside(0, 2)
    right_near(0)
    across(0, 0)
    unpack(1, 0)
    across(0, 1)
    unpack(1, 1)
    across(0, 2)
    right_far(0)
    send(0, 0)
    send(0, 1)
    unpack(1, 2)
    send(0, 2)
    for c in range(3):
        left(1, 0, c)
        beside(1, c)
    right_near(1)
    for c in range(3):
        across(1, c)
    right_far(1)
    for r in range(3):
        send(1, r)

    def convolve(m, carry):
        k, r = m // 3, lax.rem(m, 3)
        arrived(*st2(k, r))
        half = fwd[pl.ds(pl.multiple_of(256 * k, 256), 256), :]

        def one(c, carry):
            w = dot(fwd[...], side(sx[k, r, 0, c], sx[k, r, 1, c]))
            prod = []
            for h in range(2):
                g = dot(half, side(xb[c, r, h, 0], xb[c, r, h, 1]))
                gre, gim = g[:n], g[n:]
                wre, wim = w[2 * n * h : 2 * n * h + n], w[2 * n * h + n : 2 * n * h + 2 * n]
                prod += [gre * wre - gim * wim, gre * wim + gim * wre]
            v = dot(sig[...], jnp.concatenate(prod, axis=0).astype(BF)).astype(BF)
            for i in range(2):
                fs[k, r, i, c] = v[:, LANES * i : LANES * i + LANES].reshape(PIECES, 8, LANES)
            return carry

        lax.fori_loop(0, 3, one, 0, unroll=True)
        exchange(*st3(k, r))
        return carry

    lax.fori_loop(0, 6, convolve, 0)

    for r in range(3):
        sent(*[st0(r)[i] for i in (0, 1, 4)])
        for k in range(2):
            for st in (st1, st2):
                sent(*[st(k, r)[i] for i in (0, 1, 4)])
            near_copy(k, r, 1).wait_send()

    @pl.when(inner)
    def _():
        for r in range(3):
            for k in range(2):
                near_copy(k, r, 2).wait_send()

    def out_copy(k, r):
        dst = (ol, og)[k]
        return pltpu.make_async_copy(
            ob.at[k, r], dst.at[:, 0, :, pl.ds(128 * r, 128), :], out_sem.at[k, r]
        )

    for k in range(2):

        def finish(r, carry):
            arrived(*st3(k, r))
            for c in range(3):
                for j in range(2):
                    x = fr[k, r, 16 * j : 16 * j + 16, :, c].reshape(32, 8, LANES)
                    x = jnp.swapaxes(x, 0, 1)
                    for h in range(2):
                        at = 64 * h + 32 * j
                        ob[k, r, :, :, at : at + 32, LANES * c : LANES * c + LANES] = x[
                            4 * h : 4 * h + 4
                        ].reshape(2, 2, 32, LANES)
            out_copy(k, r).start()
            return carry

        lax.fori_loop(0, 3, finish, 0)

    for k in range(2):
        for r in range(3):
            sent(*[st3(k, r)[i] for i in (0, 1, 4)])
    for k in range(2):
        for r in range(3):
            out_copy(k, r).wait()


def local(lesser_green, greater_green, coulomb_blocks):
    fwd, pol, sig = dft_tables()
    any_spec = pl.BlockSpec(memory_space=pl.ANY)
    out = jax.ShapeDtypeStruct(lesser_green.shape, BF)
    tile = (8, LANES)
    dma = pltpu.SemaphoreType.DMA
    return pl.pallas_call(
        kernel,
        out_shape=(out, out),
        in_specs=[any_spec] * 6,
        out_specs=(any_spec, any_spec),
        scratch_shapes=[
            pltpu.VMEM((3, 2, 2, 2, ROWS, LANES), BF),
            pltpu.VMEM((3, 3, 2, PIECES, 2) + tile, BF),
            pltpu.VMEM((3, 3, 2, 2, PIECES) + tile, BF),
            pltpu.VMEM((2, 3, 3, 2, PIECES) + tile, BF),
            pltpu.VMEM((2, 3, 3, PIECES, 2) + tile, BF),
            pltpu.VMEM((2, 3, 3, 4, 3, 2, 64, LANES), BF),
            pltpu.VMEM((2, 3, 2, 128, 6 * ROWS), BF),
            pltpu.VMEM((6 * 128, 2 * ROWS), F32),
            pltpu.VMEM((3, 4, 3, 2, 64, LANES), BF),
            pltpu.VMEM((2, 3, PIECES, 2, 3) + tile, BF),
            pltpu.VMEM((2, 3, 2, 3, PIECES) + tile, BF),
            pltpu.VMEM((2, 3, 2, 3, PIECES) + tile, BF),
            pltpu.VMEM((2, 3, PIECES, 2, 3) + tile, BF),
            pltpu.VMEM((2, 3, 2, 2, 128, ROWS), BF),
            pltpu.VMEM((3, ROWS, 2 * ROWS), BF),
            pltpu.VMEM((3, 2 * ROWS, 2 * ROWS), BF),
            pltpu.VMEM((4 * LENGTH, 4 * NE), BF),
            pltpu.VMEM((8 * NE, 4 * LENGTH), BF),
            pltpu.VMEM((4 * NE, 4 * LENGTH), BF),
            dma((3, 2)), dma((9,)), dma((4, 6)), dma((4, 6)), dma((4, 6)), dma((2, 3, 3)),
            dma((2, 3, 3)), dma((2, 3)),
        ],
        compiler_params=pltpu.CompilerParams(
            collective_id=0, has_side_effects=True, vmem_limit_bytes=66_000_000
        ),
        name="gw",
    )(lesser_green, greater_green, coulomb_blocks, fwd, pol, sig)


def solution(mesh):
    return jax.shard_map(
        local,
        mesh=mesh,
        in_specs=(
            P("energy", "blk", None, None, None),
            P("energy", "blk", None, None, None),
            P("blk", None, None, None, None),
        ),
        out_specs=(P("energy", "blk", None, None, None), P("energy", "blk", None, None, None)),
        check_vma=False,
    )
```

```python
import functools
import math

import numpy as np
import jax
import jax.numpy as jnp
from jax import lax
from jax.experimental import pallas as pl
from jax.experimental.pallas import tpu as pltpu
from jax.sharding import PartitionSpec as P

MESH = pl.DeviceIdType.MESH
BF = jnp.bfloat16
F32 = jnp.float32
PIECES = 32
ROWS = 384
LANES = 128
NE = 64
LENGTH = 2 * NE


def dft_tables():
    f = np.arange(LENGTH)[:, None]
    e = np.arange(NE)[None, :]
    angle = 2.0 * math.pi / LENGTH * (f * e % LENGTH)
    cos, sin = np.cos(angle), np.sin(angle)
    fwd = np.zeros((2, 2, LENGTH, PIECES, 2, 2, 2))
    cs = cos.reshape(LENGTH, PIECES, 2)
    sn = sin.reshape(LENGTH, PIECES, 2)
    for k in range(2):
        fwd[k, 0, :, :, k, :, 0] = cs
        fwd[k, 0, :, :, k, :, 1] = sn
        fwd[k, 1, :, :, k, :, 0] = -sn
        fwd[k, 1, :, :, k, :, 1] = cs
    ct = cs.transpose(1, 2, 0)
    st = sn.transpose(1, 2, 0)
    scale = 1.0 / (math.sqrt(NE) * LENGTH)
    pol = np.zeros((2, PIECES, 2, 2, 2, 2, 2, LENGTH))
    for h in range(2):
        pol[0, :, h, :, 0, h, 0] = ct
        pol[0, :, h, :, 0, h, 1] = -st
        pol[0, :, h, :, 1, h, 0] = st
        pol[0, :, h, :, 1, h, 1] = ct
        pol[1, :, h, :, 0, h, 0] = ct
        pol[1, :, h, :, 0, h, 1] = st
        pol[1, :, h, :, 1, h, 0] = st
        pol[1, :, h, :, 1, h, 1] = -ct
    sig = np.zeros((PIECES, 2, 2, 2, 2, 2, LENGTH))
    for k in range(2):
        sig[:, k, :, 0, k, 0] = ct
        sig[:, k, :, 0, k, 1] = -st
        sig[:, k, :, 1, k, 0] = st
        sig[:, k, :, 1, k, 1] = ct
    as_bf = lambda a, m, n: jnp.asarray(a.reshape(m, n).astype(np.float32)).astype(BF)
    return (
        as_bf(fwd, 4 * LENGTH, 4 * NE),
        as_bf(-scale * pol, 8 * NE, 4 * LENGTH),
        as_bf(scale * sig, 4 * NE, 4 * LENGTH),
    )


def hops(step):
    dy, dz, dx = step
    return min(dy, 4 - dy) + dz + min(dx, 4 - dx)


STEPS = [((k // 8 + k // 2 % 4) % 4, k % 2, k // 2 % 4) for k in range(PIECES)]


def mirror(t):
    return (t // 8) * 8 + (1 - lax.rem(t // 4, 2)) * 4 + lax.rem(t, 4)


def dot(a, b):
    return jnp.dot(a, b, preferred_element_type=F32)


def kernel(
    lg, gg, cb, fwd_h, pol_h, sig_h, ob,
    gin, s0, xb, ps, pr, p3, lf, acc, sc, ss, sx, fs, fr, cc, rr, fwd, pol, sig,
    in_sem, tab_sem, self_sem, send_sem, recv_sem, near_send, near_recv,
):
    me = lax.axis_index("energy")
    b = lax.axis_index("blk")
    upper = b >= 2
    even = lax.rem(b, 2) == 0
    my = me // 8
    mz = lax.rem(me // 4, 2)
    mx = lax.rem(me, 4)
    inner = jnp.logical_or(b == 1, b == 2)
    core_id = {"energy": me, "blk": b + 1 - 2 * lax.rem(b, 2)}
    cross_id = {"energy": mirror(me), "blk": 3 - b}
    core_o = jnp.where(even, 2, 0)
    offsets = (1, core_o, 2 - core_o)

    ys = [8 * lax.rem(my + d, 4) for d in range(4)]
    xs = [lax.rem(mx + d, 4) for d in range(4)]
    zs = [4 * mz, 4 - 4 * mz]
    lag_zs = [jnp.where(upper, 4 - z, z) for z in zs]
    my_lag = 8 * my + lag_zs[0] + mx
    peers = []
    for dy, dz, dx in STEPS[:1] + sorted(STEPS[1:], key=hops, reverse=True):
        peers.append((ys[dy] + zs[dz] + xs[dx], ys[dy] + lag_zs[dz] + xs[dx]))

    barrier = pltpu.get_barrier_semaphore()
    for t, _ in peers[1:]:
        pl.semaphore_signal(
            barrier, inc=1, device_id={"energy": t, "blk": b}, device_id_type=MESH
        )
    pl.semaphore_signal(barrier, inc=1, device_id=core_id, device_id_type=MESH)

    @pl.when(inner)
    def _():
        pl.semaphore_signal(barrier, inc=1, device_id=cross_id, device_id_type=MESH)

    def g_copy(c, a):
        src = (lg, gg)[a]
        return pltpu.make_async_copy(
            src.at[:, 0, :, :, pl.ds(LANES * c, LANES)], gin.at[c, a], in_sem.at[c, a]
        )

    for a in range(2):
        g_copy(0, a).start()
    tables = [
        pltpu.make_async_copy(fwd_h, fwd, tab_sem.at[0]),
        pltpu.make_async_copy(pol_h, pol, tab_sem.at[1]),
        pltpu.make_async_copy(sig_h, sig, tab_sem.at[2]),
    ]
    for o in range(3):
        for r in range(2):
            tables.append(
                pltpu.make_async_copy(
                    cb.at[0, offsets[o], r],
                    cc.at[o, :, pl.ds(ROWS * r, ROWS)],
                    tab_sem.at[3 + 2 * o + r],
                )
            )

    def exchange(stage, part, source, dest, span):
        for t, lag in peers[1:]:
            pltpu.make_async_remote_copy(
                src_ref=source(t, lag), dst_ref=dest(), send_sem=send_sem.at[stage, part],
                recv_sem=recv_sem.at[stage, part], device_id={"energy": t, "blk": b},
                device_id_type=MESH,
            ).start()
        pltpu.make_async_copy(source(me, my_lag), dest(), self_sem.at[stage, part]).start()

    def arrived(stage, part, source, dest, span):
        pltpu.make_async_copy(span, span, recv_sem.at[stage, part]).wait()
        pltpu.make_async_copy(source(me, my_lag), dest(), self_sem.at[stage, part]).wait()

    def sent(stage, part, span):
        pltpu.make_async_copy(span, span, send_sem.at[stage, part]).wait()

    others = pl.ds(0, PIECES - 1)

    def st0(c):
        return (
            0, c, lambda t, lag: s0.at[c, :, :, t], lambda: xb.at[c, :, :, :, me],
            xb.at[c, :, :, :, others],
        )

    def st1(k, c):
        return (
            1, 3 * k + c, lambda t, lag: ps.at[k, c, :, :, lag], lambda: pr.at[k, c, :, me],
            pr.at[k, c, :, others],
        )

    def st2(k, r):
        return (
            2, 3 * k + r, lambda t, lag: ss.at[k, r, t], lambda: sx.at[k, r, :, :, my_lag],
            sx.at[k, r, :, :, others],
        )

    def st3(k, r):
        return (
            3, 3 * k + r, lambda t, lag: fs.at[k, r, :, :, t], lambda: fr.at[k, r, me],
            fr.at[k, r, others],
        )

    for c in range(3):
        for a in range(2):
            g_copy(c, a).wait()
        if c == 0:
            for d in range(1, 3):
                for a in range(2):
                    g_copy(d, a).start()

        def pack(i, carry):
            r, h = i // 2, lax.rem(i, 2)
            for j in range(2):
                x = gin[c, :, :, :, pl.ds(64 * i + 32 * j, 32), :].reshape(8, 32, LANES)
                s0[c, r, h, 16 * j : 16 * j + 16] = jnp.swapaxes(x, 0, 1).reshape(16, 2, 8, LANES)
            return carry

        lax.fori_loop(0, 6, pack, 0)
        if c == 0:
            pl.semaphore_wait(barrier, jnp.where(inner, PIECES + 1, PIECES))
        exchange(*st0(c))

    for copy in tables:
        copy.start()
    for copy in tables:
        copy.wait()
    for o in range(3):
        cre = cc[o, :, :ROWS].T
        cim = cc[o, :, ROWS:].T
        rr[o, :ROWS, :ROWS] = cre
        rr[o, ROWS:, ROWS:] = cre
        rr[o, ROWS:, :ROWS] = cim
        rr[o, :ROWS, ROWS:] = -cim

    n = LENGTH

    def side(x0, x1):
        return jnp.concatenate([x0.reshape(256, LANES), x1.reshape(256, LANES)], axis=1)

    def polarize(c, carry):
        arrived(*st0(c))

        def one(r, carry):
            cross = []
            for h in range(2):
                y = dot(fwd[...], side(xb[c, r, h, 0], xb[c, r, h, 1]))
                lre, lim, gre, gim = y[:n], y[n : 2 * n], y[2 * n : 3 * n], y[3 * n :]
                cross += [lre * gre + lim * gim, lim * gre - lre * gim]
            p = dot(pol[...], jnp.concatenate(cross, axis=0).astype(BF)).astype(BF)
            for k in range(2):
                for i in range(2):
                    ps[k, c, r, i] = p[
                        256 * k : 256 * k + 256, LANES * i : LANES * i + LANES
                    ].reshape(PIECES, 8, LANES)
            return carry

        lax.fori_loop(0, 3, one, 0, unroll=True)
        exchange(*st1(0, c))
        return carry

    lax.fori_loop(0, 3, polarize, 0)

    exchange(*st1(1, 0))

    def near_copy(k, c, slot):
        return pltpu.make_async_remote_copy(
            src_ref=p3.at[k, 0, c], dst_ref=p3.at[k, slot, c], send_sem=near_send.at[k, slot, c],
            recv_sem=near_recv.at[k, slot, c], device_id=core_id if slot == 1 else cross_id,
            device_id_type=MESH,
        )

    def unpack(k, c):
        arrived(*st1(k, c))
        for r in range(3):
            for j in range(2):
                x = pr[k, c, r, 16 * j : 16 * j + 16].reshape(32, 8, LANES)
                x = jnp.swapaxes(x, 0, 1)
                for h in range(2):
                    p3[k, 0, c, :, r, h, 32 * j : 32 * j + 32, :] = x[4 * h : 4 * h + 4]

        @pl.when(inner)
        def _():
            near_copy(k, c, 2).start()

        near_copy(k, c, 1).start()

    def left(k, o, c):
        for q in range(2):
            pre = p3[k, o, c, 2 * q].reshape(ROWS, LANES)
            pim = p3[k, o, c, 2 * q + 1].reshape(ROWS, LANES)
            rhs = jnp.concatenate(
                [jnp.concatenate([pre, pim], axis=1), jnp.concatenate([-pim, pre], axis=1)], axis=0
            )
            v = dot(cc[o], rhs).astype(BF)
            for p in range(2):
                at = 2 * ROWS * o + ROWS * p + LANES * c
                for r in range(3):
                    lf[k, r, q, :, at : at + LANES] = v[
                        128 * r : 128 * r + 128, LANES * p : LANES * p + LANES
                    ]

    def beside(k, c):
        near_copy(k, c, 1).wait_recv()
        left(k, 1, c)

    def across(k, c):
        @pl.when(inner)
        def _():
            near_copy(k, c, 2).wait_recv()
            left(k, 2, c)

    def right_near(k):
        for m in range(3):
            acc[:, 256 * m : 256 * m + 256] = dot(
                lf[k, :, :, :, : 4 * ROWS].reshape(6 * 128, 4 * ROWS),
                rr[:2, :, 256 * m : 256 * m + 256].reshape(4 * ROWS, 256),
            )

    def right_far(k):
        def emit(m, v):
            v = v.astype(BF)
            for h in range(2):
                part, c = divmod(2 * m + h, 3)
                for r in range(3):
                    for q in range(2):
                        at = 256 * r + 128 * q
                        sc[c, 2 * q + part, r] = v[
                            at : at + 128, LANES * h : LANES * h + LANES
                        ].reshape(2, 64, LANES)

        @pl.when(inner)
        def _():
            for m in range(3):
                emit(
                    m,
                    acc[:, 256 * m : 256 * m + 256]
                    + dot(
                        lf[k, :, :, :, 4 * ROWS :].reshape(6 * 128, 2 * ROWS),
                        rr[2, :, 256 * m : 256 * m + 256],
                    ),
                )

        @pl.when(jnp.logical_not(inner))
        def _():
            for m in range(3):
                emit(m, acc[:, 256 * m : 256 * m + 256])

    def send(k, r):
        for c in range(3):
            for j in range(2):
                x = jnp.concatenate(
                    [sc[c, :, r, h, 32 * j : 32 * j + 32, :] for h in range(2)], axis=0
                )
                ss[k, r, 16 * j : 16 * j + 16, :, c] = jnp.swapaxes(x, 0, 1).reshape(
                    16, 2, 8, LANES
                )
        exchange(*st2(k, r))

    unpack(0, 0)
    exchange(*st1(1, 1))
    unpack(0, 1)
    exchange(*st1(1, 2))
    left(0, 0, 0)
    left(0, 0, 1)
    beside(0, 0)
    unpack(0, 2)
    left(0, 0, 2)
    beside(0, 1)
    beside(0, 2)
    right_near(0)
    across(0, 0)
    unpack(1, 0)
    across(0, 1)
    unpack(1, 1)
    across(0, 2)
    right_far(0)
    send(0, 0)
    send(0, 1)
    unpack(1, 2)
    send(0, 2)
    for c in range(3):
        left(1, 0, c)
        beside(1, c)
    right_near(1)
    for c in range(3):
        across(1, c)
    right_far(1)
    for r in range(3):
        send(1, r)

    def convolve(m, carry):
        k, r = m // 3, lax.rem(m, 3)
        arrived(*st2(k, r))
        half = fwd[pl.ds(pl.multiple_of(256 * k, 256), 256), :]

        def one(c, carry):
            w = dot(fwd[...], side(sx[k, r, 0, c], sx[k, r, 1, c]))
            prod = []
            for h in range(2):
                g = dot(half, side(xb[c, r, h, 0], xb[c, r, h, 1]))
                gre, gim = g[:n], g[n:]
                wre, wim = w[2 * n * h : 2 * n * h + n], w[2 * n * h + n : 2 * n * h + 2 * n]
                prod += [gre * wre - gim * wim, gre * wim + gim * wre]
            v = dot(sig[...], jnp.concatenate(prod, axis=0).astype(BF)).astype(BF)
            for i in range(2):
                fs[k, r, i, c] = v[:, LANES * i : LANES * i + LANES].reshape(PIECES, 8, LANES)
            return carry

        lax.fori_loop(0, 3, one, 0, unroll=True)
        exchange(*st3(k, r))
        return carry

    lax.fori_loop(0, 6, convolve, 0)

    for r in range(3):
        sent(*[st0(r)[i] for i in (0, 1, 4)])
        for k in range(2):
            for st in (st1, st2):
                sent(*[st(k, r)[i] for i in (0, 1, 4)])
            near_copy(k, r, 1).wait_send()

    @pl.when(inner)
    def _():
        for r in range(3):
            for k in range(2):
                near_copy(k, r, 2).wait_send()

    for k in range(2):

        def finish(r, carry):
            arrived(*st3(k, r))
            for c in range(3):
                for j in range(2):
                    x = fr[k, r, 16 * j : 16 * j + 16, :, c].reshape(32, 8, LANES)
                    x = jnp.swapaxes(x, 0, 1)
                    for h in range(2):
                        at = 64 * h + 32 * j
                        ob[k, r, :, :, at : at + 32, LANES * c : LANES * c + LANES] = x[
                            4 * h : 4 * h + 4
                        ].reshape(2, 2, 32, LANES)
            return carry

        lax.fori_loop(0, 3, finish, 0)

    for k in range(2):
        for r in range(3):
            sent(*[st3(k, r)[i] for i in (0, 1, 4)])


def write_out(ob, ol, og, sem):
    copies = [
        pltpu.make_async_copy(
            ob.at[k, r], (ol, og)[k].at[:, 0, :, pl.ds(128 * r, 128), :], sem.at[k, r]
        )
        for k in range(2)
        for r in range(3)
    ]
    for copy in copies:
        copy.start()
    for copy in copies:
        copy.wait()


def local(lesser_green, greater_green, coulomb_blocks):
    fwd, pol, sig = dft_tables()
    any_spec = pl.BlockSpec(memory_space=pl.ANY)
    out = jax.ShapeDtypeStruct(lesser_green.shape, BF)
    tile = (8, LANES)
    dma = pltpu.SemaphoreType.DMA
    held = pl.pallas_call(
        kernel,
        out_shape=pltpu.VMEM((2, 3, 2, 2, 128, ROWS), BF),
        in_specs=[any_spec] * 6,
        out_specs=pl.BlockSpec(memory_space=pltpu.VMEM),
        scratch_shapes=[
            pltpu.VMEM((3, 2, 2, 2, ROWS, LANES), BF),
            pltpu.VMEM((3, 3, 2, PIECES, 2) + tile, BF),
            pltpu.VMEM((3, 3, 2, 2, PIECES) + tile, BF),
            pltpu.VMEM((2, 3, 3, 2, PIECES) + tile, BF),
            pltpu.VMEM((2, 3, 3, PIECES, 2) + tile, BF),
            pltpu.VMEM((2, 3, 3, 4, 3, 2, 64, LANES), BF),
            pltpu.VMEM((2, 3, 2, 128, 6 * ROWS), BF),
            pltpu.VMEM((6 * 128, 2 * ROWS), F32),
            pltpu.VMEM((3, 4, 3, 2, 64, LANES), BF),
            pltpu.VMEM((2, 3, PIECES, 2, 3) + tile, BF),
            pltpu.VMEM((2, 3, 2, 3, PIECES) + tile, BF),
            pltpu.VMEM((2, 3, 2, 3, PIECES) + tile, BF),
            pltpu.VMEM((2, 3, PIECES, 2, 3) + tile, BF),
            pltpu.VMEM((3, ROWS, 2 * ROWS), BF),
            pltpu.VMEM((3, 2 * ROWS, 2 * ROWS), BF),
            pltpu.VMEM((4 * LENGTH, 4 * NE), BF),
            pltpu.VMEM((8 * NE, 4 * LENGTH), BF),
            pltpu.VMEM((4 * NE, 4 * LENGTH), BF),
            dma((3, 2)), dma((9,)), dma((4, 6)), dma((4, 6)), dma((4, 6)), dma((2, 3, 3)),
            dma((2, 3, 3)),
        ],
        compiler_params=pltpu.CompilerParams(
            collective_id=0, has_side_effects=True, vmem_limit_bytes=60_000_000
        ),
        name="gw",
    )(lesser_green, greater_green, coulomb_blocks, fwd, pol, sig)
    return pl.pallas_call(
        write_out,
        out_shape=(out, out),
        in_specs=[any_spec],
        out_specs=(any_spec, any_spec),
        scratch_shapes=[dma((2, 3))],
        compiler_params=pltpu.CompilerParams(vmem_limit_bytes=1_000_000),
        name="out",
    )(held)


def solution(mesh):
    return jax.shard_map(
        local,
        mesh=mesh,
        in_specs=(
            P("energy", "blk", None, None, None),
            P("energy", "blk", None, None, None),
            P("blk", None, None, None, None),
        ),
        out_specs=(P("energy", "blk", None, None, None), P("energy", "blk", None, None, None)),
        check_vma=False,
    )
```

```python
import functools
import math

import numpy as np
import jax
import jax.numpy as jnp
from jax import lax
from jax.experimental import pallas as pl
from jax.experimental.pallas import tpu as pltpu
from jax.sharding import PartitionSpec as P

MESH = pl.DeviceIdType.MESH
BF = jnp.bfloat16
F32 = jnp.float32
PIECES = 32
ROWS = 384
LANES = 128
NE = 64
LENGTH = 2 * NE


def dft_tables():
    f = np.arange(LENGTH)[:, None]
    e = np.arange(NE)[None, :]
    angle = 2.0 * math.pi / LENGTH * (f * e % LENGTH)
    cos, sin = np.cos(angle), np.sin(angle)
    fwd = np.zeros((2, 2, LENGTH, PIECES, 2, 2, 2))
    cs = cos.reshape(LENGTH, PIECES, 2)
    sn = sin.reshape(LENGTH, PIECES, 2)
    for k in range(2):
        fwd[k, 0, :, :, k, :, 0] = cs
        fwd[k, 0, :, :, k, :, 1] = sn
        fwd[k, 1, :, :, k, :, 0] = -sn
        fwd[k, 1, :, :, k, :, 1] = cs
    ct = cs.transpose(1, 2, 0)
    st = sn.transpose(1, 2, 0)
    scale = 1.0 / (math.sqrt(NE) * LENGTH)
    pol = np.zeros((2, PIECES, 2, 2, 2, 2, 2, LENGTH))
    for h in range(2):
        pol[0, :, h, :, 0, h, 0] = ct
        pol[0, :, h, :, 0, h, 1] = -st
        pol[0, :, h, :, 1, h, 0] = st
        pol[0, :, h, :, 1, h, 1] = ct
        pol[1, :, h, :, 0, h, 0] = ct
        pol[1, :, h, :, 0, h, 1] = st
        pol[1, :, h, :, 1, h, 0] = st
        pol[1, :, h, :, 1, h, 1] = -ct
    sig = np.zeros((PIECES, 2, 2, 2, 2, 2, LENGTH))
    for k in range(2):
        sig[:, k, :, 0, k, 0] = ct
        sig[:, k, :, 0, k, 1] = -st
        sig[:, k, :, 1, k, 0] = st
        sig[:, k, :, 1, k, 1] = ct
    as_bf = lambda a, m, n: jnp.asarray(a.reshape(m, n).astype(np.float32)).astype(BF)
    return (
        as_bf(fwd, 4 * LENGTH, 4 * NE),
        as_bf(-scale * pol, 8 * NE, 4 * LENGTH),
        as_bf(scale * sig, 4 * NE, 4 * LENGTH),
    )


def hops(step):
    dy, dz, dx = step
    return min(dy, 4 - dy) + dz + min(dx, 4 - dx)


STEPS = [((k // 8 + k // 2 % 4) % 4, k % 2, k // 2 % 4) for k in range(PIECES)]


FIRST = (0, 1, 8, 3, 2, 24, 16, 4, 9, 11, 25, 5, 12)


def mirror(t):
    return (t // 8) * 8 + (1 - lax.rem(t // 4, 2)) * 4 + lax.rem(t, 4)


def dot(a, b):
    return jnp.dot(a, b, preferred_element_type=F32)


def kernel(
    lg, gg, cb, fwd_h, pol_h, sig_h, ob,
    gin, s0, xb, ps, pr, p3, lf, acc, sc, ss, sx, fs, fr, cc, rr, fwd, pol, sig,
    in_sem, tab_sem, self_sem, send_sem, recv_sem, near_send, near_recv, go_sem, met_sem,
):
    me = lax.axis_index("energy")
    b = lax.axis_index("blk")
    upper = b >= 2
    even = lax.rem(b, 2) == 0
    my = me // 8
    mz = lax.rem(me // 4, 2)
    mx = lax.rem(me, 4)
    inner = jnp.logical_or(b == 1, b == 2)
    core_id = {"energy": me, "blk": b + 1 - 2 * lax.rem(b, 2)}
    cross_id = {"energy": mirror(me), "blk": 3 - b}
    core_o = jnp.where(even, 2, 0)
    offsets = (1, core_o, 2 - core_o)

    ys = [8 * lax.rem(my + d, 4) for d in range(4)]
    xs = [lax.rem(mx + d, 4) for d in range(4)]
    zs = [4 * mz, 4 - 4 * mz]
    lag_zs = [jnp.where(upper, 4 - z, z) for z in zs]
    my_lag = 8 * my + lag_zs[0] + mx
    peers = []
    for dy, dz, dx in STEPS[:1] + sorted(STEPS[1:], key=hops, reverse=True):
        peers.append((ys[dy] + zs[dz] + xs[dx], ys[dy] + lag_zs[dz] + xs[dx]))

    barrier = pltpu.get_barrier_semaphore()
    for t, _ in peers[1:]:
        pl.semaphore_signal(
            barrier, inc=1, device_id={"energy": t, "blk": b}, device_id_type=MESH
        )
    pl.semaphore_signal(barrier, inc=1, device_id=core_id, device_id_type=MESH)

    @pl.when(b == 1)
    def _():
        pl.semaphore_signal(barrier, inc=1, device_id=cross_id, device_id_type=MESH)

    def g_copy(c, a):
        src = (lg, gg)[a]
        return pltpu.make_async_copy(
            src.at[:, 0, :, :, pl.ds(LANES * c, LANES)], gin.at[c, a], in_sem.at[c, a]
        )

    for a in range(2):
        g_copy(0, a).start()
    tables = [
        pltpu.make_async_copy(fwd_h, fwd, tab_sem.at[0]),
        pltpu.make_async_copy(pol_h, pol, tab_sem.at[1]),
        pltpu.make_async_copy(sig_h, sig, tab_sem.at[2]),
    ]
    for o in range(3):
        for r in range(2):
            tables.append(
                pltpu.make_async_copy(
                    cb.at[0, offsets[o], r],
                    cc.at[o, :, pl.ds(ROWS * r, ROWS)],
                    tab_sem.at[3 + 2 * o + r],
                )
            )

    def exchange(stage, part, source, dest, span):
        def one(t, lag):
            pltpu.make_async_remote_copy(
                src_ref=source(t, lag), dst_ref=dest(), send_sem=send_sem.at[stage, part],
                recv_sem=recv_sem.at[stage, part], device_id={"energy": t, "blk": b},
                device_id_type=MESH,
            ).start()

        if stage == 3:
            for t in FIRST:

                @pl.when(me != t)
                def _():
                    one(t, t)

            for t, lag in peers[1:]:

                @pl.when(functools.reduce(jnp.logical_and, [t != f for f in FIRST]))
                def _():
                    one(t, lag)
        else:
            for t, lag in peers[1:]:
                one(t, lag)
        pltpu.make_async_copy(source(me, my_lag), dest(), self_sem.at[stage, part]).start()

    def arrived(stage, part, source, dest, span):
        pltpu.make_async_copy(span, span, recv_sem.at[stage, part]).wait()
        pltpu.make_async_copy(source(me, my_lag), dest(), self_sem.at[stage, part]).wait()

    def sent(stage, part, span):
        pltpu.make_async_copy(span, span, send_sem.at[stage, part]).wait()

    others = pl.ds(0, PIECES - 1)

    def st0(c):
        return (
            0, c, lambda t, lag: s0.at[c, :, :, t], lambda: xb.at[c, :, :, :, me],
            xb.at[c, :, :, :, others],
        )

    def st1(k, c):
        return (
            1, 3 * k + c, lambda t, lag: ps.at[k, c, :, :, lag], lambda: pr.at[k, c, :, me],
            pr.at[k, c, :, others],
        )

    def st2(k, r):
        return (
            2, 3 * k + r, lambda t, lag: ss.at[k, r, t], lambda: sx.at[k, r, :, :, my_lag],
            sx.at[k, r, :, :, others],
        )

    def st3(k, r):
        return (
            3, 3 * k + r, lambda t, lag: fs.at[k, r, :, :, t], lambda: fr.at[k, r, me],
            fr.at[k, r, others],
        )

    for c in range(3):
        for a in range(2):
            g_copy(c, a).wait()
        if c == 0:
            for d in range(1, 3):
                for a in range(2):
                    g_copy(d, a).start()

        def pack(i, carry):
            r, h = i // 2, lax.rem(i, 2)
            for j in range(2):
                x = gin[c, :, :, :, pl.ds(64 * i + 32 * j, 32), :].reshape(8, 32, LANES)
                s0[c, r, h, 16 * j : 16 * j + 16] = jnp.swapaxes(x, 0, 1).reshape(16, 2, 8, LANES)
            return carry

        lax.fori_loop(0, 6, pack, 0)
        if c == 0:
            pl.semaphore_wait(barrier, jnp.where(b == 2, PIECES + 1, PIECES))

            @pl.when(b == 2)
            def _():
                pl.semaphore_signal(met_sem, inc=1, device_id=cross_id, device_id_type=MESH)

        if c == 1:

            @pl.when(b == 3)
            def _():
                pl.semaphore_wait(go_sem, 1)

        exchange(*st0(c))

    for copy in tables:
        copy.start()
    for copy in tables:
        copy.wait()
    for o in range(3):
        cre = cc[o, :, :ROWS].T
        cim = cc[o, :, ROWS:].T
        rr[o, :ROWS, :ROWS] = cre
        rr[o, ROWS:, ROWS:] = cre
        rr[o, ROWS:, :ROWS] = cim
        rr[o, :ROWS, ROWS:] = -cim

    n = LENGTH

    def side(x0, x1):
        return jnp.concatenate([x0.reshape(256, LANES), x1.reshape(256, LANES)], axis=1)

    def polarize(c, carry):
        arrived(*st0(c))

        @pl.when(jnp.logical_and(c == 0, b == 2))
        def _():
            pl.semaphore_signal(go_sem, inc=1, device_id=core_id, device_id_type=MESH)

        def one(r, carry):
            cross = []
            for h in range(2):
                y = dot(fwd[...], side(xb[c, r, h, 0], xb[c, r, h, 1]))
                lre, lim, gre, gim = y[:n], y[n : 2 * n], y[2 * n : 3 * n], y[3 * n :]
                cross += [lre * gre + lim * gim, lim * gre - lre * gim]
            p = dot(pol[...], jnp.concatenate(cross, axis=0).astype(BF)).astype(BF)
            for k in range(2):
                for i in range(2):
                    ps[k, c, r, i] = p[
                        256 * k : 256 * k + 256, LANES * i : LANES * i + LANES
                    ].reshape(PIECES, 8, LANES)
            return carry

        lax.fori_loop(0, 3, one, 0, unroll=True)
        exchange(*st1(0, c))
        return carry

    lax.fori_loop(0, 3, polarize, 0)

    def near_copy(k, c, slot):
        return pltpu.make_async_remote_copy(
            src_ref=p3.at[k, 0, c], dst_ref=p3.at[k, slot, c], send_sem=near_send.at[k, slot, c],
            recv_sem=near_recv.at[k, slot, c], device_id=core_id if slot == 1 else cross_id,
            device_id_type=MESH,
        )

    def unpack(k, c):
        arrived(*st1(k, c))
        for r in range(3):
            for j in range(2):
                x = pr[k, c, r, 16 * j : 16 * j + 16].reshape(32, 8, LANES)
                x = jnp.swapaxes(x, 0, 1)
                for h in range(2):
                    p3[k, 0, c, :, r, h, 32 * j : 32 * j + 32, :] = x[4 * h : 4 * h + 4]

        @pl.when(inner)
        def _():
            near_copy(k, c, 2).start()

        near_copy(k, c, 1).start()

    def left(k, o, c):
        for q in range(2):
            pre = p3[k, o, c, 2 * q].reshape(ROWS, LANES)
            pim = p3[k, o, c, 2 * q + 1].reshape(ROWS, LANES)
            rhs = jnp.concatenate(
                [jnp.concatenate([pre, pim], axis=1), jnp.concatenate([-pim, pre], axis=1)], axis=0
            )
            v = dot(cc[o], rhs).astype(BF)
            for p in range(2):
                at = 2 * ROWS * o + ROWS * p + LANES * c
                for r in range(3):
                    lf[k, r, q, :, at : at + LANES] = v[
                        128 * r : 128 * r + 128, LANES * p : LANES * p + LANES
                    ]

    def beside(k, c):
        near_copy(k, c, 1).wait_recv()
        left(k, 1, c)

    def across(k, c):
        @pl.when(inner)
        def _():
            near_copy(k, c, 2).wait_recv()
            left(k, 2, c)

    def right_near(k):
        for m in range(3):
            acc[:, 256 * m : 256 * m + 256] = dot(
                lf[k, :, :, :, : 4 * ROWS].reshape(6 * 128, 4 * ROWS),
                rr[:2, :, 256 * m : 256 * m + 256].reshape(4 * ROWS, 256),
            )

    def right_far(k):
        def emit(m, v):
            v = v.astype(BF)
            for h in range(2):
                part, c = divmod(2 * m + h, 3)
                for r in range(3):
                    for q in range(2):
                        at = 256 * r + 128 * q
                        sc[c, 2 * q + part, r] = v[
                            at : at + 128, LANES * h : LANES * h + LANES
                        ].reshape(2, 64, LANES)

        @pl.when(inner)
        def _():
            for m in range(3):
                emit(
                    m,
                    acc[:, 256 * m : 256 * m + 256]
                    + dot(
                        lf[k, :, :, :, 4 * ROWS :].reshape(6 * 128, 2 * ROWS),
                        rr[2, :, 256 * m : 256 * m + 256],
                    ),
                )

        @pl.when(jnp.logical_not(inner))
        def _():
            for m in range(3):
                emit(m, acc[:, 256 * m : 256 * m + 256])

    def send(k, r):
        for c in range(3):
            for j in range(2):
                x = jnp.concatenate(
                    [sc[c, :, r, h, 32 * j : 32 * j + 32, :] for h in range(2)], axis=0
                )
                ss[k, r, 16 * j : 16 * j + 16, :, c] = jnp.swapaxes(x, 0, 1).reshape(
                    16, 2, 8, LANES
                )
        exchange(*st2(k, r))

    @pl.when(b == 1)
    def _():
        pl.semaphore_wait(met_sem, 1)

    unpack(0, 0)
    exchange(*st1(1, 0))
    unpack(0, 1)
    exchange(*st1(1, 1))
    left(0, 0, 0)
    left(0, 0, 1)
    beside(0, 0)
    unpack(0, 2)
    exchange(*st1(1, 2))
    left(0, 0, 2)
    beside(0, 1)
    beside(0, 2)
    right_near(0)
    across(0, 0)
    unpack(1, 0)
    across(0, 1)
    unpack(1, 1)
    across(0, 2)
    right_far(0)
    send(0, 0)
    send(0, 1)
    unpack(1, 2)
    send(0, 2)
    for c in range(3):
        left(1, 0, c)
        beside(1, c)
    right_near(1)
    for c in range(3):
        across(1, c)
    right_far(1)
    for r in range(3):
        send(1, r)

    def convolve(m, carry):
        k, r = m // 3, lax.rem(m, 3)
        arrived(*st2(k, r))
        half = fwd[pl.ds(pl.multiple_of(256 * k, 256), 256), :]

        def one(c, carry):
            w = dot(fwd[...], side(sx[k, r, 0, c], sx[k, r, 1, c]))
            prod = []
            for h in range(2):
                g = dot(half, side(xb[c, r, h, 0], xb[c, r, h, 1]))
                gre, gim = g[:n], g[n:]
                wre, wim = w[2 * n * h : 2 * n * h + n], w[2 * n * h + n : 2 * n * h + 2 * n]
                prod += [gre * wre - gim * wim, gre * wim + gim * wre]
            v = dot(sig[...], jnp.concatenate(prod, axis=0).astype(BF)).astype(BF)
            for i in range(2):
                fs[k, r, i, c] = v[:, LANES * i : LANES * i + LANES].reshape(PIECES, 8, LANES)
            return carry

        lax.fori_loop(0, 3, one, 0, unroll=True)
        exchange(*st3(k, r))
        return carry

    lax.fori_loop(0, 6, convolve, 0)

    for r in range(3):
        sent(*[st0(r)[i] for i in (0, 1, 4)])
        for k in range(2):
            for st in (st1, st2):
                sent(*[st(k, r)[i] for i in (0, 1, 4)])
            near_copy(k, r, 1).wait_send()

    @pl.when(inner)
    def _():
        for r in range(3):
            for k in range(2):
                near_copy(k, r, 2).wait_send()

    for k in range(2):

        def finish(r, carry):
            arrived(*st3(k, r))
            for c in range(3):
                for j in range(2):
                    x = fr[k, r, 16 * j : 16 * j + 16, :, c].reshape(32, 8, LANES)
                    x = jnp.swapaxes(x, 0, 1)
                    for h in range(2):
                        at = 64 * h + 32 * j
                        ob[k, r, :, :, at : at + 32, LANES * c : LANES * c + LANES] = x[
                            4 * h : 4 * h + 4
                        ].reshape(2, 2, 32, LANES)
            return carry

        lax.fori_loop(0, 3, finish, 0)

    for k in range(2):
        for r in range(3):
            sent(*[st3(k, r)[i] for i in (0, 1, 4)])


def write_out(ob, ol, og, sem):
    copies = [
        pltpu.make_async_copy(
            ob.at[k, r], (ol, og)[k].at[:, 0, :, pl.ds(128 * r, 128), :], sem.at[k, r]
        )
        for k in range(2)
        for r in range(3)
    ]
    for copy in copies:
        copy.start()
    for copy in copies:
        copy.wait()


def local(lesser_green, greater_green, coulomb_blocks):
    fwd, pol, sig = dft_tables()
    any_spec = pl.BlockSpec(memory_space=pl.ANY)
    out = jax.ShapeDtypeStruct(lesser_green.shape, BF)
    tile = (8, LANES)
    dma = pltpu.SemaphoreType.DMA
    held = pl.pallas_call(
        kernel,
        out_shape=pltpu.VMEM((2, 3, 2, 2, 128, ROWS), BF),
        in_specs=[any_spec] * 6,
        out_specs=pl.BlockSpec(memory_space=pltpu.VMEM),
        scratch_shapes=[
            pltpu.VMEM((3, 2, 2, 2, ROWS, LANES), BF),
            pltpu.VMEM((3, 3, 2, PIECES, 2) + tile, BF),
            pltpu.VMEM((3, 3, 2, 2, PIECES) + tile, BF),
            pltpu.VMEM((2, 3, 3, 2, PIECES) + tile, BF),
            pltpu.VMEM((2, 3, 3, PIECES, 2) + tile, BF),
            pltpu.VMEM((2, 3, 3, 4, 3, 2, 64, LANES), BF),
            pltpu.VMEM((2, 3, 2, 128, 6 * ROWS), BF),
            pltpu.VMEM((6 * 128, 2 * ROWS), F32),
            pltpu.VMEM((3, 4, 3, 2, 64, LANES), BF),
            pltpu.VMEM((2, 3, PIECES, 2, 3) + tile, BF),
            pltpu.VMEM((2, 3, 2, 3, PIECES) + tile, BF),
            pltpu.VMEM((2, 3, 2, 3, PIECES) + tile, BF),
            pltpu.VMEM((2, 3, PIECES, 2, 3) + tile, BF),
            pltpu.VMEM((3, ROWS, 2 * ROWS), BF),
            pltpu.VMEM((3, 2 * ROWS, 2 * ROWS), BF),
            pltpu.VMEM((4 * LENGTH, 4 * NE), BF),
            pltpu.VMEM((8 * NE, 4 * LENGTH), BF),
            pltpu.VMEM((4 * NE, 4 * LENGTH), BF),
            dma((3, 2)), dma((9,)), dma((4, 6)), dma((4, 6)), dma((4, 6)), dma((2, 3, 3)),
            dma((2, 3, 3)), pltpu.SemaphoreType.REGULAR, pltpu.SemaphoreType.REGULAR,
        ],
        compiler_params=pltpu.CompilerParams(
            collective_id=0, has_side_effects=True, vmem_limit_bytes=60_000_000
        ),
        name="gw",
    )(lesser_green, greater_green, coulomb_blocks, fwd, pol, sig)
    return pl.pallas_call(
        write_out,
        out_shape=(out, out),
        in_specs=[any_spec],
        out_specs=(any_spec, any_spec),
        scratch_shapes=[dma((2, 3))],
        compiler_params=pltpu.CompilerParams(vmem_limit_bytes=1_000_000),
        name="out",
    )(held)


def solution(mesh):
    return jax.shard_map(
        local,
        mesh=mesh,
        in_specs=(
            P("energy", "blk", None, None, None),
            P("energy", "blk", None, None, None),
            P("blk", None, None, None, None),
        ),
        out_specs=(P("energy", "blk", None, None, None), P("energy", "blk", None, None, None)),
        check_vma=False,
    )
```

```python
import functools
import math

import numpy as np
import jax
import jax.numpy as jnp
from jax import lax
from jax.experimental import pallas as pl
from jax.experimental.pallas import tpu as pltpu
from jax.sharding import PartitionSpec as P

MESH = pl.DeviceIdType.MESH
BF = jnp.bfloat16
F32 = jnp.float32
PIECES = 32
ROWS = 384
LANES = 128
NE = 64
LENGTH = 2 * NE


def dft_tables():
    f = np.arange(LENGTH)[:, None]
    e = np.arange(NE)[None, :]
    angle = 2.0 * math.pi / LENGTH * (f * e % LENGTH)
    cos, sin = np.cos(angle), np.sin(angle)
    fwd = np.zeros((2, 2, LENGTH, PIECES, 2, 2, 2))
    cs = cos.reshape(LENGTH, PIECES, 2)
    sn = sin.reshape(LENGTH, PIECES, 2)
    for k in range(2):
        fwd[k, 0, :, :, k, :, 0] = cs
        fwd[k, 0, :, :, k, :, 1] = sn
        fwd[k, 1, :, :, k, :, 0] = -sn
        fwd[k, 1, :, :, k, :, 1] = cs
    ct = cs.transpose(1, 2, 0)
    st = sn.transpose(1, 2, 0)
    scale = 1.0 / (math.sqrt(NE) * LENGTH)
    pol = np.zeros((2, PIECES, 2, 2, 2, 2, 2, LENGTH))
    for h in range(2):
        pol[0, :, h, :, 0, h, 0] = ct
        pol[0, :, h, :, 0, h, 1] = -st
        pol[0, :, h, :, 1, h, 0] = st
        pol[0, :, h, :, 1, h, 1] = ct
        pol[1, :, h, :, 0, h, 0] = ct
        pol[1, :, h, :, 0, h, 1] = st
        pol[1, :, h, :, 1, h, 0] = st
        pol[1, :, h, :, 1, h, 1] = -ct
    sig = np.zeros((PIECES, 2, 2, 2, 2, 2, LENGTH))
    for k in range(2):
        sig[:, k, :, 0, k, 0] = ct
        sig[:, k, :, 0, k, 1] = -st
        sig[:, k, :, 1, k, 0] = st
        sig[:, k, :, 1, k, 1] = ct
    as_bf = lambda a, m, n: jnp.asarray(a.reshape(m, n).astype(np.float32)).astype(BF)
    return (
        as_bf(fwd, 4 * LENGTH, 4 * NE),
        as_bf(-scale * pol, 8 * NE, 4 * LENGTH),
        as_bf(scale * sig, 4 * NE, 4 * LENGTH),
    )


def hops(step):
    dy, dz, dx = step
    return min(dy, 4 - dy) + dz + min(dx, 4 - dx)


STEPS = [((k // 8 + k // 2 % 4) % 4, k % 2, k // 2 % 4) for k in range(PIECES)]


FIRST = (0, 1, 8, 3, 2, 24, 16, 4, 9, 11, 25, 5, 12)


def mirror(t):
    return (t // 8) * 8 + (1 - lax.rem(t // 4, 2)) * 4 + lax.rem(t, 4)


def dot(a, b):
    return jnp.dot(a, b, preferred_element_type=F32)


def kernel(
    lg, gg, cb, fwd_h, pol_h, sig_h, ob,
    gin, s0, xb, ps, pr, p3, lf, acc, sc, ss, sx, fs, fr, cc, rr, fwd, pol, sig,
    in_sem, tab_sem, self_sem, send_sem, recv_sem, near_send, near_recv, go_sem, met_sem,
):
    me = lax.axis_index("energy")
    b = lax.axis_index("blk")
    upper = b >= 2
    even = lax.rem(b, 2) == 0
    my = me // 8
    mz = lax.rem(me // 4, 2)
    mx = lax.rem(me, 4)
    inner = jnp.logical_or(b == 1, b == 2)
    core_id = {"energy": me, "blk": b + 1 - 2 * lax.rem(b, 2)}
    cross_id = {"energy": mirror(me), "blk": 3 - b}
    core_o = jnp.where(even, 2, 0)
    offsets = (1, core_o, 2 - core_o)

    ys = [8 * lax.rem(my + d, 4) for d in range(4)]
    xs = [lax.rem(mx + d, 4) for d in range(4)]
    zs = [4 * mz, 4 - 4 * mz]
    lag_zs = [jnp.where(upper, 4 - z, z) for z in zs]
    my_lag = 8 * my + lag_zs[0] + mx
    peers = []
    for dy, dz, dx in STEPS[:1] + sorted(STEPS[1:], key=hops, reverse=True):
        peers.append((ys[dy] + zs[dz] + xs[dx], ys[dy] + lag_zs[dz] + xs[dx]))

    barrier = pltpu.get_barrier_semaphore()
    for t, _ in peers[1:]:
        pl.semaphore_signal(
            barrier, inc=1, device_id={"energy": t, "blk": b}, device_id_type=MESH
        )
    pl.semaphore_signal(barrier, inc=1, device_id=core_id, device_id_type=MESH)

    @pl.when(b == 1)
    def _():
        pl.semaphore_signal(barrier, inc=1, device_id=cross_id, device_id_type=MESH)

    def g_copy(c, a):
        src = (lg, gg)[a]
        return pltpu.make_async_copy(
            src.at[:, 0, :, :, pl.ds(LANES * c, LANES)], gin.at[c, a], in_sem.at[c, a]
        )

    for a in range(2):
        g_copy(0, a).start()
    tables = [
        pltpu.make_async_copy(fwd_h, fwd, tab_sem.at[0]),
        pltpu.make_async_copy(pol_h, pol, tab_sem.at[1]),
        pltpu.make_async_copy(sig_h, sig, tab_sem.at[2]),
    ]
    for o in range(3):
        for r in range(2):
            tables.append(
                pltpu.make_async_copy(
                    cb.at[0, offsets[o], r],
                    cc.at[o, :, pl.ds(ROWS * r, ROWS)],
                    tab_sem.at[3 + 2 * o + r],
                )
            )

    def exchange(stage, part, source, dest, span):
        def one(t, lag):
            pltpu.make_async_remote_copy(
                src_ref=source(t, lag), dst_ref=dest(), send_sem=send_sem.at[stage, part],
                recv_sem=recv_sem.at[stage, part], device_id={"energy": t, "blk": b},
                device_id_type=MESH,
            ).start()

        if stage == 3:
            for t in FIRST:

                @pl.when(me != t)
                def _():
                    one(t, t)

            for t, lag in peers[1:]:

                @pl.when(functools.reduce(jnp.logical_and, [t != f for f in FIRST]))
                def _():
                    one(t, lag)
        else:
            for t, lag in peers[1:]:
                one(t, lag)
        pltpu.make_async_copy(source(me, my_lag), dest(), self_sem.at[stage, part]).start()

    def arrived(stage, part, source, dest, span):
        pltpu.make_async_copy(span, span, recv_sem.at[stage, part]).wait()
        pltpu.make_async_copy(source(me, my_lag), dest(), self_sem.at[stage, part]).wait()

    def sent(stage, part, span):
        pltpu.make_async_copy(span, span, send_sem.at[stage, part]).wait()

    others = pl.ds(0, PIECES - 1)

    def st0(c):
        return (
            0, c, lambda t, lag: s0.at[c, :, :, t], lambda: xb.at[c, :, :, :, me],
            xb.at[c, :, :, :, others],
        )

    def st1(k, c):
        return (
            1, 3 * k + c, lambda t, lag: ps.at[k, c, :, :, lag], lambda: pr.at[k, c, :, me],
            pr.at[k, c, :, others],
        )

    def st2(k, r):
        return (
            2, 3 * k + r, lambda t, lag: ss.at[k, r, t], lambda: sx.at[k, r, :, :, my_lag],
            sx.at[k, r, :, :, others],
        )

    def st3(k, r):
        return (
            3, 3 * k + r, lambda t, lag: fs.at[k, r, :, :, t], lambda: fr.at[k, r, me],
            fr.at[k, r, others],
        )

    for c in range(3):
        for a in range(2):
            g_copy(c, a).wait()
        if c == 0:
            for d in range(1, 3):
                for a in range(2):
                    g_copy(d, a).start()

        def pack(i, carry):
            r, h = i // 2, lax.rem(i, 2)
            for j in range(2):
                x = gin[c, :, :, :, pl.ds(64 * i + 32 * j, 32), :].reshape(8, 32, LANES)
                s0[c, r, h, 16 * j : 16 * j + 16] = jnp.swapaxes(x, 0, 1).reshape(16, 2, 8, LANES)
            return carry

        lax.fori_loop(0, 6, pack, 0)
        if c == 0:
            pl.semaphore_wait(barrier, jnp.where(b == 2, PIECES + 1, PIECES))

            @pl.when(b == 2)
            def _():
                pl.semaphore_signal(met_sem, inc=1, device_id=cross_id, device_id_type=MESH)

        if c == 1:

            @pl.when(b == 3)
            def _():
                pl.semaphore_wait(go_sem, 1)

        exchange(*st0(c))

    for copy in tables:
        copy.start()
    for copy in tables:
        copy.wait()
    for o in range(3):
        cre = cc[o, :, :ROWS].T
        cim = cc[o, :, ROWS:].T
        rr[o, :ROWS, :ROWS] = cre
        rr[o, ROWS:, ROWS:] = cre
        rr[o, ROWS:, :ROWS] = cim
        rr[o, :ROWS, ROWS:] = -cim

    n = LENGTH

    def side(x0, x1):
        return jnp.concatenate([x0.reshape(256, LANES), x1.reshape(256, LANES)], axis=1)

    def polarize(c, carry):
        arrived(*st0(c))

        @pl.when(jnp.logical_and(c == 0, b == 2))
        def _():
            pl.semaphore_signal(go_sem, inc=1, device_id=core_id, device_id_type=MESH)

        def one(r, carry):
            cross = []
            for h in range(2):
                y = dot(fwd[...], side(xb[c, r, h, 0], xb[c, r, h, 1]))
                lre, lim, gre, gim = y[:n], y[n : 2 * n], y[2 * n : 3 * n], y[3 * n :]
                cross += [lre * gre + lim * gim, lim * gre - lre * gim]
            p = dot(pol[...], jnp.concatenate(cross, axis=0).astype(BF)).astype(BF)
            for k in range(2):
                for i in range(2):
                    ps[k, c, r, i] = p[
                        256 * k : 256 * k + 256, LANES * i : LANES * i + LANES
                    ].reshape(PIECES, 8, LANES)
            return carry

        lax.fori_loop(0, 3, one, 0, unroll=True)
        exchange(*st1(0, c))
        return carry

    lax.fori_loop(0, 3, polarize, 0)

    def near_copy(k, c, slot):
        return pltpu.make_async_remote_copy(
            src_ref=p3.at[k, 0, c], dst_ref=p3.at[k, slot, c], send_sem=near_send.at[k, slot, c],
            recv_sem=near_recv.at[k, slot, c], device_id=core_id if slot == 1 else cross_id,
            device_id_type=MESH,
        )

    def unpack(k, c):
        arrived(*st1(k, c))
        for r in range(3):
            for j in range(2):
                x = pr[k, c, r, 16 * j : 16 * j + 16].reshape(32, 8, LANES)
                x = jnp.swapaxes(x, 0, 1)
                for h in range(2):
                    p3[k, 0, c, :, r, h, 32 * j : 32 * j + 32, :] = x[4 * h : 4 * h + 4]

        @pl.when(inner)
        def _():
            near_copy(k, c, 2).start()

        near_copy(k, c, 1).start()

    def left(k, o, c):
        for q in range(2):
            pre = p3[k, o, c, 2 * q].reshape(ROWS, LANES)
            pim = p3[k, o, c, 2 * q + 1].reshape(ROWS, LANES)
            rhs = jnp.concatenate(
                [jnp.concatenate([pre, pim], axis=1), jnp.concatenate([-pim, pre], axis=1)], axis=0
            )
            v = dot(cc[o], rhs).astype(BF)
            for p in range(2):
                at = 2 * ROWS * o + ROWS * p + LANES * c
                for r in range(3):
                    lf[k, r, q, :, at : at + LANES] = v[
                        128 * r : 128 * r + 128, LANES * p : LANES * p + LANES
                    ]

    def beside(k, c):
        near_copy(k, c, 1).wait_recv()
        left(k, 1, c)

    def across(k, c):
        @pl.when(inner)
        def _():
            near_copy(k, c, 2).wait_recv()
            left(k, 2, c)

    def right_near(k):
        for m in range(3):
            acc[:, 256 * m : 256 * m + 256] = dot(
                lf[k, :, :, :, : 4 * ROWS].reshape(6 * 128, 4 * ROWS),
                rr[:2, :, 256 * m : 256 * m + 256].reshape(4 * ROWS, 256),
            )

    def right_far(k):
        def emit(m, v):
            v = v.astype(BF)
            for h in range(2):
                part, c = divmod(2 * m + h, 3)
                for r in range(3):
                    for q in range(2):
                        at = 256 * r + 128 * q
                        sc[c, 2 * q + part, r] = v[
                            at : at + 128, LANES * h : LANES * h + LANES
                        ].reshape(2, 64, LANES)

        @pl.when(inner)
        def _():
            for m in range(3):
                emit(
                    m,
                    acc[:, 256 * m : 256 * m + 256]
                    + dot(
                        lf[k, :, :, :, 4 * ROWS :].reshape(6 * 128, 2 * ROWS),
                        rr[2, :, 256 * m : 256 * m + 256],
                    ),
                )

        @pl.when(jnp.logical_not(inner))
        def _():
            for m in range(3):
                emit(m, acc[:, 256 * m : 256 * m + 256])

    def send(k, r):
        for c in range(3):
            for j in range(2):
                x = jnp.concatenate(
                    [sc[c, :, r, h, 32 * j : 32 * j + 32, :] for h in range(2)], axis=0
                )
                ss[k, r, 16 * j : 16 * j + 16, :, c] = jnp.swapaxes(x, 0, 1).reshape(
                    16, 2, 8, LANES
                )
        exchange(*st2(k, r))

    @pl.when(b == 1)
    def _():
        pl.semaphore_wait(met_sem, 1)

    unpack(0, 0)
    exchange(*st1(1, 0))
    unpack(0, 1)
    exchange(*st1(1, 1))
    left(0, 0, 0)
    left(0, 0, 1)
    beside(0, 0)
    unpack(0, 2)
    exchange(*st1(1, 2))
    left(0, 0, 2)
    beside(0, 1)
    beside(0, 2)
    right_near(0)
    across(0, 0)
    unpack(1, 0)
    across(0, 1)
    unpack(1, 1)
    across(0, 2)
    right_far(0)
    send(0, 0)
    send(0, 1)
    unpack(1, 2)
    send(0, 2)
    for c in range(3):
        left(1, 0, c)
        beside(1, c)
    right_near(1)
    for c in range(3):
        across(1, c)
    right_far(1)
    for r in range(3):
        send(1, r)

    def convolve(m, carry):
        k, r = m // 3, lax.rem(m, 3)
        arrived(*st2(k, r))
        half = fwd[pl.ds(pl.multiple_of(256 * k, 256), 256), :]

        def one(c, carry):
            w = dot(fwd[...], side(sx[k, r, 0, c], sx[k, r, 1, c]))
            prod = []
            for h in range(2):
                g = dot(half, side(xb[c, r, h, 0], xb[c, r, h, 1]))
                gre, gim = g[:n], g[n:]
                wre, wim = w[2 * n * h : 2 * n * h + n], w[2 * n * h + n : 2 * n * h + 2 * n]
                prod += [gre * wre - gim * wim, gre * wim + gim * wre]
            v = dot(sig[...], jnp.concatenate(prod, axis=0).astype(BF)).astype(BF)
            for i in range(2):
                fs[k, r, i, c] = v[:, LANES * i : LANES * i + LANES].reshape(PIECES, 8, LANES)
            return carry

        lax.fori_loop(0, 3, one, 0, unroll=True)
        exchange(*st3(k, r))
        return carry

    lax.fori_loop(0, 6, convolve, 0)

    for r in range(3):
        sent(*[st0(r)[i] for i in (0, 1, 4)])
        for k in range(2):
            for st in (st1, st2):
                sent(*[st(k, r)[i] for i in (0, 1, 4)])
            near_copy(k, r, 1).wait_send()

    @pl.when(inner)
    def _():
        for r in range(3):
            for k in range(2):
                near_copy(k, r, 2).wait_send()

    def finish(k, r):
        arrived(*st3(k, r))
        for c in range(3):
            for j in range(2):
                x = fr[k, r, 16 * j : 16 * j + 16, :, c].reshape(32, 8, LANES)
                x = jnp.swapaxes(x, 0, 1)
                for h in range(2):
                    at = pl.multiple_of(128 * r + 64 * h + 32 * j, 32)
                    ob[k, :, :, pl.ds(at, 32), LANES * c : LANES * c + LANES] = x[
                        4 * h : 4 * h + 4
                    ].reshape(2, 2, 32, LANES)

    def most(m, carry):
        finish(m // 3, lax.rem(m, 3))
        return carry

    lax.fori_loop(0, 5, most, 0)
    for k in range(2):
        for r in range(3):
            sent(*[st3(k, r)[i] for i in (0, 1, 4)])
    finish(1, 2)


def write_out(ob, ol, og, sem):
    copies = [
        pltpu.make_async_copy(ob.at[k], (ol, og)[k].at[:, 0], sem.at[k]) for k in range(2)
    ]
    for copy in copies:
        copy.start()
    for copy in copies:
        copy.wait()


def local(lesser_green, greater_green, coulomb_blocks):
    fwd, pol, sig = dft_tables()
    any_spec = pl.BlockSpec(memory_space=pl.ANY)
    out = jax.ShapeDtypeStruct(lesser_green.shape, BF)
    tile = (8, LANES)
    dma = pltpu.SemaphoreType.DMA
    held = pl.pallas_call(
        kernel,
        out_shape=pltpu.VMEM((2, 2, 2, ROWS, ROWS), BF),
        in_specs=[any_spec] * 6,
        out_specs=pl.BlockSpec(memory_space=pltpu.VMEM),
        scratch_shapes=[
            pltpu.VMEM((3, 2, 2, 2, ROWS, LANES), BF),
            pltpu.VMEM((3, 3, 2, PIECES, 2) + tile, BF),
            pltpu.VMEM((3, 3, 2, 2, PIECES) + tile, BF),
            pltpu.VMEM((2, 3, 3, 2, PIECES) + tile, BF),
            pltpu.VMEM((2, 3, 3, PIECES, 2) + tile, BF),
            pltpu.VMEM((2, 3, 3, 4, 3, 2, 64, LANES), BF),
            pltpu.VMEM((2, 3, 2, 128, 6 * ROWS), BF),
            pltpu.VMEM((6 * 128, 2 * ROWS), F32),
            pltpu.VMEM((3, 4, 3, 2, 64, LANES), BF),
            pltpu.VMEM((2, 3, PIECES, 2, 3) + tile, BF),
            pltpu.VMEM((2, 3, 2, 3, PIECES) + tile, BF),
            pltpu.VMEM((2, 3, 2, 3, PIECES) + tile, BF),
            pltpu.VMEM((2, 3, PIECES, 2, 3) + tile, BF),
            pltpu.VMEM((3, ROWS, 2 * ROWS), BF),
            pltpu.VMEM((3, 2 * ROWS, 2 * ROWS), BF),
            pltpu.VMEM((4 * LENGTH, 4 * NE), BF),
            pltpu.VMEM((8 * NE, 4 * LENGTH), BF),
            pltpu.VMEM((4 * NE, 4 * LENGTH), BF),
            dma((3, 2)), dma((9,)), dma((4, 6)), dma((4, 6)), dma((4, 6)), dma((2, 3, 3)),
            dma((2, 3, 3)), pltpu.SemaphoreType.REGULAR, pltpu.SemaphoreType.REGULAR,
        ],
        compiler_params=pltpu.CompilerParams(
            collective_id=0, has_side_effects=True, vmem_limit_bytes=60_000_000
        ),
        name="gw",
    )(lesser_green, greater_green, coulomb_blocks, fwd, pol, sig)
    return pl.pallas_call(
        write_out,
        out_shape=(out, out),
        in_specs=[any_spec],
        out_specs=(any_spec, any_spec),
        scratch_shapes=[dma((2,))],
        compiler_params=pltpu.CompilerParams(vmem_limit_bytes=1_000_000),
        name="out",
    )(held)


def solution(mesh):
    return jax.shard_map(
        local,
        mesh=mesh,
        in_specs=(
            P("energy", "blk", None, None, None),
            P("energy", "blk", None, None, None),
            P("blk", None, None, None, None),
        ),
        out_specs=(P("energy", "blk", None, None, None), P("energy", "blk", None, None, None)),
        check_vma=False,
    )
```

```python
import functools
import math

import numpy as np
import jax
import jax.numpy as jnp
from jax import lax
from jax.experimental import pallas as pl
from jax.experimental.pallas import tpu as pltpu
from jax.sharding import PartitionSpec as P

MESH = pl.DeviceIdType.MESH
BF = jnp.bfloat16
F32 = jnp.float32
PIECES = 32
ROWS = 384
LANES = 128
NE = 64
LENGTH = 2 * NE


def dft_tables():
    f = np.arange(LENGTH)[:, None]
    e = np.arange(NE)[None, :]
    angle = 2.0 * math.pi / LENGTH * (f * e % LENGTH)
    cos, sin = np.cos(angle), np.sin(angle)
    fwd = np.zeros((2, 2, LENGTH, PIECES, 2, 2, 2))
    cs = cos.reshape(LENGTH, PIECES, 2)
    sn = sin.reshape(LENGTH, PIECES, 2)
    for k in range(2):
        fwd[k, 0, :, :, k, :, 0] = cs
        fwd[k, 0, :, :, k, :, 1] = sn
        fwd[k, 1, :, :, k, :, 0] = -sn
        fwd[k, 1, :, :, k, :, 1] = cs
    ct = cs.transpose(1, 2, 0)
    st = sn.transpose(1, 2, 0)
    scale = 1.0 / (math.sqrt(NE) * LENGTH)
    pol = np.zeros((2, PIECES, 2, 2, 2, 2, 2, LENGTH))
    for h in range(2):
        pol[0, :, h, :, 0, h, 0] = ct
        pol[0, :, h, :, 0, h, 1] = -st
        pol[0, :, h, :, 1, h, 0] = st
        pol[0, :, h, :, 1, h, 1] = ct
        pol[1, :, h, :, 0, h, 0] = ct
        pol[1, :, h, :, 0, h, 1] = st
        pol[1, :, h, :, 1, h, 0] = st
        pol[1, :, h, :, 1, h, 1] = -ct
    sig = np.zeros((PIECES, 2, 2, 2, 2, 2, LENGTH))
    for k in range(2):
        sig[:, k, :, 0, k, 0] = ct
        sig[:, k, :, 0, k, 1] = -st
        sig[:, k, :, 1, k, 0] = st
        sig[:, k, :, 1, k, 1] = ct
    as_bf = lambda a, m, n: jnp.asarray(a.reshape(m, n).astype(np.float32)).astype(BF)
    return (
        as_bf(fwd, 4 * LENGTH, 4 * NE),
        as_bf(-scale * pol, 8 * NE, 4 * LENGTH),
        as_bf(scale * sig, 4 * NE, 4 * LENGTH),
    )


def hops(step):
    dy, dz, dx = step
    return min(dy, 4 - dy) + dz + min(dx, 4 - dx)


STEPS = [((k // 8 + k // 2 % 4) % 4, k % 2, k // 2 % 4) for k in range(PIECES)]


FIRST = (0, 1, 8, 3, 2, 24, 16, 4, 9, 11, 25, 5, 12)


def mirror(t):
    return (t // 8) * 8 + (1 - lax.rem(t // 4, 2)) * 4 + lax.rem(t, 4)


def dot(a, b):
    return jnp.dot(a, b, preferred_element_type=F32)


def kernel(
    lg, gg, cb, fwd_h, pol_h, sig_h, ob,
    gin, s0, xb, ps, pr, p3, lf, acc, sc, ss, sx, fs, fr, cc, rr, fwd, pol, sig,
    in_sem, tab_sem, self_sem, send_sem, recv_sem, near_send, near_recv, go_sem, met_sem, turn_sem,
):
    me = lax.axis_index("energy")
    b = lax.axis_index("blk")
    upper = b >= 2
    even = lax.rem(b, 2) == 0
    my = me // 8
    mz = lax.rem(me // 4, 2)
    mx = lax.rem(me, 4)
    inner = jnp.logical_or(b == 1, b == 2)
    core_id = {"energy": me, "blk": b + 1 - 2 * lax.rem(b, 2)}
    cross_id = {"energy": mirror(me), "blk": 3 - b}
    core_o = jnp.where(even, 2, 0)
    offsets = (1, core_o, 2 - core_o)

    ys = [8 * lax.rem(my + d, 4) for d in range(4)]
    xs = [lax.rem(mx + d, 4) for d in range(4)]
    zs = [4 * mz, 4 - 4 * mz]
    lag_zs = [jnp.where(upper, 4 - z, z) for z in zs]
    my_lag = 8 * my + lag_zs[0] + mx
    peers = []
    for dy, dz, dx in STEPS[:1] + sorted(STEPS[1:], key=hops, reverse=True):
        peers.append((ys[dy] + zs[dz] + xs[dx], ys[dy] + lag_zs[dz] + xs[dx]))

    barrier = pltpu.get_barrier_semaphore()
    for t, _ in peers[1:]:
        pl.semaphore_signal(
            barrier, inc=1, device_id={"energy": t, "blk": b}, device_id_type=MESH
        )
    pl.semaphore_signal(barrier, inc=1, device_id=core_id, device_id_type=MESH)

    @pl.when(b == 1)
    def _():
        pl.semaphore_signal(barrier, inc=1, device_id=cross_id, device_id_type=MESH)

    def g_copy(c, a):
        src = (lg, gg)[a]
        return pltpu.make_async_copy(
            src.at[:, 0, :, :, pl.ds(LANES * c, LANES)], gin.at[c, a], in_sem.at[c, a]
        )

    for a in range(2):
        g_copy(0, a).start()
    tables = [
        pltpu.make_async_copy(fwd_h, fwd, tab_sem.at[0]),
        pltpu.make_async_copy(pol_h, pol, tab_sem.at[1]),
        pltpu.make_async_copy(sig_h, sig, tab_sem.at[2]),
    ]
    for o in range(3):
        for r in range(2):
            tables.append(
                pltpu.make_async_copy(
                    cb.at[0, offsets[o], r],
                    cc.at[o, :, pl.ds(ROWS * r, ROWS)],
                    tab_sem.at[3 + 2 * o + r],
                )
            )

    def exchange(stage, part, source, dest, span):
        def one(t, lag):
            pltpu.make_async_remote_copy(
                src_ref=source(t, lag), dst_ref=dest(), send_sem=send_sem.at[stage, part],
                recv_sem=recv_sem.at[stage, part], device_id={"energy": t, "blk": b},
                device_id_type=MESH,
            ).start()

        if stage == 3:
            for t in FIRST:

                @pl.when(me != t)
                def _():
                    one(t, t)

            for t, lag in peers[1:]:

                @pl.when(functools.reduce(jnp.logical_and, [t != f for f in FIRST]))
                def _():
                    one(t, lag)
        else:
            for t, lag in peers[1:]:
                one(t, lag)
        pltpu.make_async_copy(source(me, my_lag), dest(), self_sem.at[stage, part]).start()

    def arrived(stage, part, source, dest, span):
        pltpu.make_async_copy(span, span, recv_sem.at[stage, part]).wait()
        pltpu.make_async_copy(source(me, my_lag), dest(), self_sem.at[stage, part]).wait()

    def sent(stage, part, span):
        pltpu.make_async_copy(span, span, send_sem.at[stage, part]).wait()

    others = pl.ds(0, PIECES - 1)

    def st0(c):
        return (
            0, c, lambda t, lag: s0.at[c, :, :, t], lambda: xb.at[c, :, :, :, me],
            xb.at[c, :, :, :, others],
        )

    def st1(k, c):
        return (
            1, 3 * k + c, lambda t, lag: ps.at[k, c, :, :, lag], lambda: pr.at[k, c, :, me],
            pr.at[k, c, :, others],
        )

    def st2(k, r):
        return (
            2, 3 * k + r, lambda t, lag: ss.at[k, r, t], lambda: sx.at[k, r, :, :, my_lag],
            sx.at[k, r, :, :, others],
        )

    def st3(k, r):
        return (
            3, 3 * k + r, lambda t, lag: fs.at[k, r, :, :, t], lambda: fr.at[k, r, me],
            fr.at[k, r, others],
        )

    for c in range(3):
        for a in range(2):
            g_copy(c, a).wait()
        if c == 0:
            for d in range(1, 3):
                for a in range(2):
                    g_copy(d, a).start()

        def pack(i, carry):
            r, h = i // 2, lax.rem(i, 2)
            for j in range(2):
                x = gin[c, :, :, :, pl.ds(64 * i + 32 * j, 32), :].reshape(8, 32, LANES)
                s0[c, r, h, 16 * j : 16 * j + 16] = jnp.swapaxes(x, 0, 1).reshape(16, 2, 8, LANES)
            return carry

        lax.fori_loop(0, 6, pack, 0)
        if c == 0:
            pl.semaphore_wait(barrier, jnp.where(b == 2, PIECES + 1, PIECES))

            @pl.when(b == 2)
            def _():
                pl.semaphore_signal(met_sem, inc=1, device_id=cross_id, device_id_type=MESH)

        if c == 1:

            @pl.when(b == 3)
            def _():
                pl.semaphore_wait(go_sem, 1)

        exchange(*st0(c))

    for copy in tables:
        copy.start()
    for copy in tables:
        copy.wait()
    for o in range(3):
        cre = cc[o, :, :ROWS].T
        cim = cc[o, :, ROWS:].T
        rr[o, :ROWS, :ROWS] = cre
        rr[o, ROWS:, ROWS:] = cre
        rr[o, ROWS:, :ROWS] = cim
        rr[o, :ROWS, ROWS:] = -cim

    n = LENGTH

    def side(x0, x1):
        return jnp.concatenate([x0.reshape(256, LANES), x1.reshape(256, LANES)], axis=1)

    def polarize(c, carry):
        arrived(*st0(c))

        @pl.when(jnp.logical_and(c == 0, b == 2))
        def _():
            pl.semaphore_signal(go_sem, inc=1, device_id=core_id, device_id_type=MESH)

        def one(r, carry):
            cross = []
            for h in range(2):
                y = dot(fwd[...], side(xb[c, r, h, 0], xb[c, r, h, 1]))
                lre, lim, gre, gim = y[:n], y[n : 2 * n], y[2 * n : 3 * n], y[3 * n :]
                cross += [lre * gre + lim * gim, lim * gre - lre * gim]
            p = dot(pol[...], jnp.concatenate(cross, axis=0).astype(BF)).astype(BF)
            for k in range(2):
                for i in range(2):
                    ps[k, c, r, i] = p[
                        256 * k : 256 * k + 256, LANES * i : LANES * i + LANES
                    ].reshape(PIECES, 8, LANES)
            return carry

        lax.fori_loop(0, 3, one, 0, unroll=True)
        exchange(*st1(0, c))
        return carry

    lax.fori_loop(0, 3, polarize, 0)

    def near_copy(k, c, slot):
        return pltpu.make_async_remote_copy(
            src_ref=p3.at[k, 0, c], dst_ref=p3.at[k, slot, c], send_sem=near_send.at[k, slot, c],
            recv_sem=near_recv.at[k, slot, c], device_id=core_id if slot == 1 else cross_id,
            device_id_type=MESH,
        )

    def unpack(k, c):
        arrived(*st1(k, c))
        for r in range(3):
            for j in range(2):
                x = pr[k, c, r, 16 * j : 16 * j + 16].reshape(32, 8, LANES)
                x = jnp.swapaxes(x, 0, 1)
                for h in range(2):
                    p3[k, 0, c, :, r, h, 32 * j : 32 * j + 32, :] = x[4 * h : 4 * h + 4]

        @pl.when(inner)
        def _():
            near_copy(k, c, 2).start()

        near_copy(k, c, 1).start()

    def left(k, o, c):
        for q in range(2):
            pre = p3[k, o, c, 2 * q].reshape(ROWS, LANES)
            pim = p3[k, o, c, 2 * q + 1].reshape(ROWS, LANES)
            rhs = jnp.concatenate(
                [jnp.concatenate([pre, pim], axis=1), jnp.concatenate([-pim, pre], axis=1)], axis=0
            )
            v = dot(cc[o], rhs).astype(BF)
            for p in range(2):
                at = 2 * ROWS * o + ROWS * p + LANES * c
                for r in range(3):
                    lf[k, r, q, :, at : at + LANES] = v[
                        128 * r : 128 * r + 128, LANES * p : LANES * p + LANES
                    ]

    def beside(k, c):
        near_copy(k, c, 1).wait_recv()
        left(k, 1, c)

    def across(k, c):
        @pl.when(inner)
        def _():
            near_copy(k, c, 2).wait_recv()
            left(k, 2, c)

    def right_near(k):
        for m in range(3):
            acc[:, 256 * m : 256 * m + 256] = dot(
                lf[k, :, :, :, : 4 * ROWS].reshape(6 * 128, 4 * ROWS),
                rr[:2, :, 256 * m : 256 * m + 256].reshape(4 * ROWS, 256),
            )

    def right_far(k):
        def emit(m, v):
            v = v.astype(BF)
            for h in range(2):
                part, c = divmod(2 * m + h, 3)
                for r in range(3):
                    for q in range(2):
                        at = 256 * r + 128 * q
                        sc[c, 2 * q + part, r] = v[
                            at : at + 128, LANES * h : LANES * h + LANES
                        ].reshape(2, 64, LANES)

        @pl.when(inner)
        def _():
            for m in range(3):
                emit(
                    m,
                    acc[:, 256 * m : 256 * m + 256]
                    + dot(
                        lf[k, :, :, :, 4 * ROWS :].reshape(6 * 128, 2 * ROWS),
                        rr[2, :, 256 * m : 256 * m + 256],
                    ),
                )

        @pl.when(jnp.logical_not(inner))
        def _():
            for m in range(3):
                emit(m, acc[:, 256 * m : 256 * m + 256])

    def send(k, r):
        for c in range(3):
            for j in range(2):
                x = jnp.concatenate(
                    [sc[c, :, r, h, 32 * j : 32 * j + 32, :] for h in range(2)], axis=0
                )
                ss[k, r, 16 * j : 16 * j + 16, :, c] = jnp.swapaxes(x, 0, 1).reshape(
                    16, 2, 8, LANES
                )
        exchange(*st2(k, r))

    @pl.when(b == 1)
    def _():
        pl.semaphore_wait(met_sem, 1)

    unpack(0, 0)
    exchange(*st1(1, 0))
    unpack(0, 1)
    exchange(*st1(1, 1))
    left(0, 0, 0)
    left(0, 0, 1)
    beside(0, 0)
    unpack(0, 2)
    exchange(*st1(1, 2))
    left(0, 0, 2)
    beside(0, 1)
    beside(0, 2)
    right_near(0)
    across(0, 0)
    unpack(1, 0)
    across(0, 1)
    unpack(1, 1)
    across(0, 2)
    right_far(0)
    send(0, 0)
    send(0, 1)
    unpack(1, 2)
    send(0, 2)
    for c in range(3):
        left(1, 0, c)
        beside(1, c)
    right_near(1)
    for c in range(3):
        across(1, c)
    right_far(1)
    for r in range(3):
        send(1, r)

    def convolve(m, carry):
        k, r = m // 3, lax.rem(m, 3)

        @pl.when(jnp.logical_and(m == 3, jnp.logical_not(inner)))
        def _():
            pl.semaphore_wait(turn_sem, 1)

        arrived(*st2(k, r))

        @pl.when(jnp.logical_and(m == 3, inner))
        def _():
            pl.semaphore_signal(turn_sem, inc=1, device_id=core_id, device_id_type=MESH)

        half = fwd[pl.ds(pl.multiple_of(256 * k, 256), 256), :]

        def one(c, carry):
            w = dot(fwd[...], side(sx[k, r, 0, c], sx[k, r, 1, c]))
            prod = []
            for h in range(2):
                g = dot(half, side(xb[c, r, h, 0], xb[c, r, h, 1]))
                gre, gim = g[:n], g[n:]
                wre, wim = w[2 * n * h : 2 * n * h + n], w[2 * n * h + n : 2 * n * h + 2 * n]
                prod += [gre * wre - gim * wim, gre * wim + gim * wre]
            v = dot(sig[...], jnp.concatenate(prod, axis=0).astype(BF)).astype(BF)
            for i in range(2):
                fs[k, r, i, c] = v[:, LANES * i : LANES * i + LANES].reshape(PIECES, 8, LANES)
            return carry

        lax.fori_loop(0, 3, one, 0, unroll=True)
        exchange(*st3(k, r))
        return carry

    lax.fori_loop(0, 6, convolve, 0)

    for r in range(3):
        sent(*[st0(r)[i] for i in (0, 1, 4)])
        for k in range(2):
            for st in (st1, st2):
                sent(*[st(k, r)[i] for i in (0, 1, 4)])
            near_copy(k, r, 1).wait_send()

    @pl.when(inner)
    def _():
        for r in range(3):
            for k in range(2):
                near_copy(k, r, 2).wait_send()

    def finish(k, r):
        arrived(*st3(k, r))
        for c in range(3):
            for j in range(2):
                x = fr[k, r, 16 * j : 16 * j + 16, :, c].reshape(32, 8, LANES)
                x = jnp.swapaxes(x, 0, 1)
                for h in range(2):
                    at = pl.multiple_of(128 * r + 64 * h + 32 * j, 32)
                    ob[k, :, :, pl.ds(at, 32), LANES * c : LANES * c + LANES] = x[
                        4 * h : 4 * h + 4
                    ].reshape(2, 2, 32, LANES)

    def most(m, carry):
        finish(m // 3, lax.rem(m, 3))
        return carry

    lax.fori_loop(0, 5, most, 0)
    for k in range(2):
        for r in range(3):
            sent(*[st3(k, r)[i] for i in (0, 1, 4)])
    finish(1, 2)


def write_out(ob, ol, og, sem):
    copies = [
        pltpu.make_async_copy(ob.at[k], (ol, og)[k].at[:, 0], sem.at[k]) for k in range(2)
    ]
    for copy in copies:
        copy.start()
    for copy in copies:
        copy.wait()


def local(lesser_green, greater_green, coulomb_blocks):
    fwd, pol, sig = dft_tables()
    any_spec = pl.BlockSpec(memory_space=pl.ANY)
    out = jax.ShapeDtypeStruct(lesser_green.shape, BF)
    tile = (8, LANES)
    dma = pltpu.SemaphoreType.DMA
    held = pl.pallas_call(
        kernel,
        out_shape=pltpu.VMEM((2, 2, 2, ROWS, ROWS), BF),
        in_specs=[any_spec] * 6,
        out_specs=pl.BlockSpec(memory_space=pltpu.VMEM),
        scratch_shapes=[
            pltpu.VMEM((3, 2, 2, 2, ROWS, LANES), BF),
            pltpu.VMEM((3, 3, 2, PIECES, 2) + tile, BF),
            pltpu.VMEM((3, 3, 2, 2, PIECES) + tile, BF),
            pltpu.VMEM((2, 3, 3, 2, PIECES) + tile, BF),
            pltpu.VMEM((2, 3, 3, PIECES, 2) + tile, BF),
            pltpu.VMEM((2, 3, 3, 4, 3, 2, 64, LANES), BF),
            pltpu.VMEM((2, 3, 2, 128, 6 * ROWS), BF),
            pltpu.VMEM((6 * 128, 2 * ROWS), F32),
            pltpu.VMEM((3, 4, 3, 2, 64, LANES), BF),
            pltpu.VMEM((2, 3, PIECES, 2, 3) + tile, BF),
            pltpu.VMEM((2, 3, 2, 3, PIECES) + tile, BF),
            pltpu.VMEM((2, 3, 2, 3, PIECES) + tile, BF),
            pltpu.VMEM((2, 3, PIECES, 2, 3) + tile, BF),
            pltpu.VMEM((3, ROWS, 2 * ROWS), BF),
            pltpu.VMEM((3, 2 * ROWS, 2 * ROWS), BF),
            pltpu.VMEM((4 * LENGTH, 4 * NE), BF),
            pltpu.VMEM((8 * NE, 4 * LENGTH), BF),
            pltpu.VMEM((4 * NE, 4 * LENGTH), BF),
            dma((3, 2)), dma((9,)), dma((4, 6)), dma((4, 6)), dma((4, 6)), dma((2, 3, 3)),
            dma((2, 3, 3)), pltpu.SemaphoreType.REGULAR, pltpu.SemaphoreType.REGULAR,
            pltpu.SemaphoreType.REGULAR,
        ],
        compiler_params=pltpu.CompilerParams(
            collective_id=0, has_side_effects=True, vmem_limit_bytes=60_000_000
        ),
        name="gw",
    )(lesser_green, greater_green, coulomb_blocks, fwd, pol, sig)
    return pl.pallas_call(
        write_out,
        out_shape=(out, out),
        in_specs=[any_spec],
        out_specs=(any_spec, any_spec),
        scratch_shapes=[dma((2,))],
        compiler_params=pltpu.CompilerParams(vmem_limit_bytes=1_000_000),
        name="out",
    )(held)


def solution(mesh):
    return jax.shard_map(
        local,
        mesh=mesh,
        in_specs=(
            P("energy", "blk", None, None, None),
            P("energy", "blk", None, None, None),
            P("blk", None, None, None, None),
        ),
        out_specs=(P("energy", "blk", None, None, None), P("energy", "blk", None, None, None)),
        check_vma=False,
    )
```
